256 devices in a mesh: dp: 8 (over y, core), seq: 32 (over z, x).
Axes of the slice: x: 4, y: 4, z: 8, core: 2. Of those that a mesh axis runs over, the one named last changes fastest.
Arguments:
- queries: bfloat16 [8, 16384, 1024], P('dp', 'seq'), may hold values from -6 to 6
- keys: bfloat16 [8, 16384, 1024], P('dp', 'seq'), may hold values from -6 to 6
- values: bfloat16 [8, 16384, 1024], P('dp', 'seq'), may hold values from -6 to 6
- out_grad: bfloat16 [8, 16384, 2048], P('dp', 'seq'), may hold values from -6 to 6
- out_weight: bfloat16 [1024, 2048], P(('dp', 'seq')), may hold values from -0.125 to 0.125
- gain: float32 [1024], replicated, may hold values from 0.1 to 1.9
Outputs:
- query_grad: bfloat16 [8, 16384, 1024], P('dp', 'seq')
- key_grad: bfloat16 [8, 16384, 1024], P('dp', 'seq')
- value_grad: bfloat16 [8, 16384, 1024], P('dp', 'seq')
- weight_grad: float32 [1024, 2048], P(('dp', 'seq'))
- gain_grad: float32 [1024], replicated
The draws below stay inside these ranges and needn't reach their ends.
All inputs are finite; a program needn't handle non-finite values.
Results may differ from the reference program's by a relative error of at most 0.015.
Values may be sent and summed in bfloat16 or wider, within the bound.
A program may use at most 128 MiB of HBM per device.

```python
import jax
import jax.numpy as jnp
from jax import lax

D = 2048
HEADS = 8
HEAD_DIM = 128
BLOCK = 512
HD = 1024
LENGTH = 16384
BATCH = 8
ALLTOK = 131072


def steps_of(stream_key, shape, cuts, low, largest):
    level = 1.0
    for position, shards_of in cuts:
        steps = jax.random.uniform(jax.random.fold_in(jax.random.fold_in(stream_key, 6), position), (shards_of,), jnp.float32, low / len(cuts), largest / len(cuts))
        level = level * jnp.repeat(jnp.exp(steps), shape[position] // shards_of).reshape((-1,) + (1,) * (len(shape) - 1 - position))
    return level


def bell_draw(stream_key, extent, scale, bound, split=(), kind=jnp.bfloat16):
    result = scale * jax.random.normal(stream_key, extent, jnp.float32)
    if split:
        result = result * steps_of(stream_key, extent, split, -0.22, 0.18)
    return jnp.clip(result, -bound, bound).astype(kind)


def setup_inputs(seed: int = 0) -> dict:
    streams_of = jax.random.split(jax.random.key(seed), 7)
    queries = bell_draw(streams_of[0], (BATCH, LENGTH, HD), 1.0, 6.0, ((0, 8), (1, 32)))
    keys = bell_draw(streams_of[1], (BATCH, LENGTH, HD), 1.0, 6.0, ((0, 8), (1, 32)))
    values = bell_draw(streams_of[2], (BATCH, LENGTH, HD), 1.0, 6.0, ((0, 8), (1, 32)))
    out_grad = bell_draw(streams_of[3], (BATCH, LENGTH, D), 1.0, 6.0, ((0, 8), (1, 32)))
    out_weight = bell_draw(streams_of[4], (HD, D), D ** -0.5, 0.125, ((0, 256),))
    gain = jnp.clip(1.0 + 0.18 * jax.random.normal(streams_of[5], (HD,), jnp.float32), 0.1, 1.9)
    return {"queries": queries, "keys": keys, "values": values, "out_grad": out_grad, "out_weight": out_weight, "gain": gain}


norm_eps = 1e-06

def as_float(array):
    return array.astype(jnp.float32)

def causal_mask():
    places = jnp.arange(BLOCK, dtype=jnp.int32)
    return (places[None, :] <= places[:, None]).astype(jnp.float32)

def reference(queries, keys, values, out_grad, out_weight, gain):
    causal = causal_mask()
    gain_heads = gain.reshape(HEADS, HEAD_DIM)
    blocks = LENGTH // BLOCK
    block_shape = (blocks, BLOCK, HEADS, HEAD_DIM)

    def one_sequence(items):
        seq_q, seq_k, seq_v, seq_g = items
        query_blk = seq_q.reshape(block_shape)
        key_blk = seq_k.reshape(block_shape)
        value_blk = seq_v.reshape(block_shape)
        grad_blk = seq_g.reshape(blocks, BLOCK, D)

        def forward_step(carry, inputs):
            state, weight_acc, gain_acc = carry
            qx, kx, vx, gx = inputs
            state_bf = state.astype(jnp.bfloat16)
            attn_bf = (jnp.einsum('thd,shd->hts', as_float(qx), as_float(kx)) * causal[None]).astype(jnp.bfloat16)
            outputs = jnp.einsum('hts,shd->thd', as_float(attn_bf), as_float(vx)) + jnp.einsum('thd,hde->the', as_float(qx), as_float(state_bf))
            rms = jnp.sqrt(lax.optimization_barrier(jnp.mean(outputs * outputs, axis=-1, keepdims=True)) + norm_eps)
            normed = outputs / rms
            unit_bf = (normed * gain_heads[None]).astype(jnp.bfloat16)
            unit_grad = jnp.dot(gx, out_weight.T, preferred_element_type=jnp.float32).reshape(BLOCK, HEADS, HEAD_DIM)
            gain_acc = gain_acc + lax.optimization_barrier(jnp.sum(unit_grad * normed, axis=0))
            scaled = unit_grad * gain_heads[None]
            middle = lax.optimization_barrier(jnp.mean(scaled * normed, axis=-1, keepdims=True))
            attn_grad = ((scaled - normed * middle) / rms).astype(jnp.bfloat16)
            weight_acc = weight_acc + jnp.dot(unit_bf.reshape(BLOCK, HD).T, gx, preferred_element_type=jnp.float32)
            state = state + jnp.einsum('shd,she->hde', as_float(kx), as_float(vx))
            return ((state, weight_acc, gain_acc), (attn_grad, state_bf))
        start_carry = (jnp.zeros((HEADS, HEAD_DIM, HEAD_DIM), jnp.float32), jnp.zeros((HD, D), jnp.float32), jnp.zeros((HEADS, HEAD_DIM), jnp.float32))
        (state_end, weight_acc, gain_acc), (attn_grads, states_bf) = lax.scan(forward_step, start_carry, (query_blk, key_blk, value_blk, grad_blk))

        def backward_step(rev, inputs):
            qx, kx, vx, ag, sbf = inputs
            rev_bf = rev.astype(jnp.bfloat16)
            attn_bf = (jnp.einsum('thd,shd->hts', as_float(qx), as_float(kx)) * causal[None]).astype(jnp.bfloat16)
            score_grad = (jnp.einsum('the,she->hts', as_float(ag), as_float(vx)) * causal[None]).astype(jnp.bfloat16)
            query_g = jnp.einsum('hts,shd->thd', as_float(score_grad), as_float(kx)) + jnp.einsum('the,hde->thd', as_float(ag), as_float(sbf))
            key_g = jnp.einsum('hts,thd->shd', as_float(score_grad), as_float(qx)) + jnp.einsum('she,hde->shd', as_float(vx), as_float(rev_bf))
            value_g = jnp.einsum('hts,the->she', as_float(attn_bf), as_float(ag)) + jnp.einsum('shd,hde->she', as_float(kx), as_float(rev_bf))
            rev = rev + jnp.einsum('thd,the->hde', as_float(qx), as_float(ag))
            return (rev, (query_g.astype(jnp.bfloat16), key_g.astype(jnp.bfloat16), value_g.astype(jnp.bfloat16)))
        rev_zero = jnp.zeros((HEADS, HEAD_DIM, HEAD_DIM), jnp.float32)
        rev_end, (query_g, key_g, value_g) = lax.scan(backward_step, rev_zero, (query_blk, key_blk, value_blk, attn_grads, states_bf), reverse=True)
        return (query_g.reshape(LENGTH, HD), key_g.reshape(LENGTH, HD), value_g.reshape(LENGTH, HD), weight_acc, gain_acc.reshape(HD))
    query_grad, key_grad, value_grad, weight_parts, gain_parts = lax.map(one_sequence, (queries, keys, values, out_grad))
    factor = 1.0 / jnp.sqrt(jnp.float32(ALLTOK))
    weight_grad = lax.optimization_barrier(jnp.sum(weight_parts, axis=0)) * factor
    gain_grad = lax.optimization_barrier(jnp.sum(gain_parts, axis=0)) * factor
    return (query_grad, key_grad, value_grad, weight_grad, gain_grad)
```

```python
import functools

import jax
import jax.numpy as jnp
from jax import lax
from jax.experimental import pallas as pl
from jax.experimental.pallas import tpu as pltpu
from jax.sharding import PartitionSpec as P

HEADS = 8
HEAD_DIM = 128
NORM_EPS = 1e-06
XDIM = 4
YDIM = 4
CORES = 2
MESH = pl.DeviceIdType.MESH
F32 = jnp.float32
BF16 = jnp.bfloat16

NT = (((1,), (1,)), ((), ()))
TN = (((0,), (0,)), ((), ()))


def mm(a, b, dims=(((1,), (0,)), ((), ()))):
    return lax.dot_general(a, b, dims, preferred_element_type=F32)


def kernel(nz, factor, q_hbm, k_hbm, v_hbm, g_hbm, w_hbm, gain_ref,
           qo_hbm, ko_hbm, vo_hbm, wo_ref, go_ref,
           q, k, v, g, oq, ok, ov, wx, asm, wbuf, attn, outp, unit, ag, kpart, vpart,
           kvs, ra, tz, po, st, qgs, rra, rtz, rpo, rst,
           wgp, prt, ys2, yr2, ysf, yrc, ysb, yrs, fsum, wself,
           zus, zur, zds, zdr, xs, xr, gx, gz, gy, gc,
           in_s, out_s, wx_s, wx_r, wz_s, wz_r, wy_s, wy_r, wp_s, wp_r,
           sx_s, sx_r, sz_s, sz_r, sb_s, sb_r, rp_s, rp_r, ry_s, ry_r, rz_s, rz_r, rx_s, rx_r,
           gx_s, gx_r, gz_s, gz_r, gy_s, gy_r, gc_s, gc_r):
    nx = XDIM
    hx = HEADS // nx
    half = nz // 2
    me_dp = lax.axis_index("dp")
    me_seq = lax.axis_index("seq")
    y = me_dp // CORES
    c = me_dp % CORES
    z = me_seq // nx
    x = me_seq % nx
    step = 1 - 2 * c
    yf = (y + step + YDIM) % YDIM
    yb = (y - step + YDIM) % YDIM
    y2 = (y + 2) % YDIM
    zup = (z + 1) % nz
    zdn = (z + nz - 1) % nz
    tokens = q.shape[0]
    hd = HEAD_DIM
    rows = wx.shape[1]

    to_f = (yf * CORES + c, me_seq)
    to_b = (yb * CORES + c, me_seq)
    to_p = (y * CORES + 1 - c, me_seq)
    to_up = (me_dp, zup * nx + x)
    to_dn = (me_dp, zdn * nx + x)

    def to_x(j):
        return (me_dp, z * nx + j)

    pending = []

    def send(src, dst, ss, rs, dev):
        copy = pltpu.make_async_remote_copy(
            src_ref=src, dst_ref=dst, send_sem=ss, recv_sem=rs, device_id=dev, device_id_type=MESH)
        copy.start()
        pending.append(copy)

    def arrived(dst, ss, rs, dev):
        pltpu.make_async_remote_copy(
            src_ref=dst, dst_ref=dst, send_sem=ss, recv_sem=rs, device_id=dev, device_id_type=MESH).wait_recv()

    def cols(h):
        return pl.ds(pl.multiple_of(h * hd, hd), hd)

    barrier = pltpu.get_barrier_semaphore()
    peers = [to_x((x + i) % nx) for i in range(1, nx)] + [to_up, to_dn, to_f, to_b, to_p]
    for peer in peers:
        pl.semaphore_signal(barrier, inc=1, device_id=peer, device_id_type=MESH)

    loads = [pltpu.make_async_copy(a, b, in_s.at[i]) for i, (a, b) in enumerate(
        [(k_hbm.at[0], k), (v_hbm.at[0], v), (w_hbm, wx.at[x]), (q_hbm.at[0], q), (g_hbm.at[0], g)])]
    for load in loads:
        load.start()
    pl.semaphore_wait(barrier, len(peers))

    for i in range(1, nx):
        send(w_hbm, wx.at[x], wx_s.at[i], wx_r.at[x], to_x((x + i) % nx))

    loads[0].wait()
    loads[1].wait()

    def kv_head(h, _):
        kvs[h // hx, h % hx] = mm(k[:, cols(h)], v[:, cols(h)], TN).astype(BF16)
        return 0

    lax.fori_loop(0, HEADS, kv_head, 0)

    def scan_x_send(n, snd, recv):
        for i in range(1, nx):
            j = (x + i) % nx
            send(snd.at[j], recv.at[x], sx_s.at[n, i], sx_r.at[n, x], to_x(j))
        recv[x] = snd[x]

    def scan_x_sum(n, recv, ring):
        for i in range(1, nx):
            j = (x + i) % nx
            arrived(recv.at[j], sx_s.at[n, i], sx_r.at[n, j], to_x(j))
        total = recv[0].astype(F32)
        for j in range(1, nx):
            total = total + recv[j].astype(F32)
        ring[z] = total.astype(BF16)

    def ring_start(buf, blk, ss, rs):
        send(buf.at[blk(z)], buf.at[blk(z)], ss.at[0, 0], rs.at[z], to_up)
        if half > 1:
            send(buf.at[blk(z)], buf.at[blk(z)], ss.at[1, 0], rs.at[z], to_dn)

    def ring_step(buf, blk, ss, rs, n):
        up = (z + nz - n) % nz
        arrived(buf.at[blk(up)], ss.at[0, n], rs.at[up], to_up)
        if n < half:
            send(buf.at[blk(up)], buf.at[blk(up)], ss.at[0, n], rs.at[up], to_up)
            dn = (z + n) % nz
            arrived(buf.at[blk(dn)], ss.at[1, n], rs.at[dn], to_dn)
            if n < half - 1:
                send(buf.at[blk(dn)], buf.at[blk(dn)], ss.at[1, n], rs.at[dn], to_dn)

    def scan_finish(n, recv, ring, out, state, reverse):
        acc = jnp.zeros((hx, hd, hd), F32)
        for zz in range(nz):
            keep = (z < zz) if reverse else (zz < z)
            acc = acc + ring[zz].astype(F32) * keep.astype(F32)
        for j in (range(nx - 1, -1, -1) if reverse else range(nx)):
            out[j] = acc.astype(BF16)
            acc = acc + recv[j].astype(F32)
        for i in range(1, nx):
            j = (x + i) % nx
            send(out.at[j], state.at[x], sb_s.at[n, i], sb_r.at[n, x], to_x(j))
        state[x] = out[x]

    def scan_wait(n, state):
        for i in range(1, nx):
            j = (x + i) % nx
            arrived(state.at[j], sb_s.at[n, i], sb_r.at[n, j], to_x(j))

    scan_x_send(0, kvs, ra)

    for i in range(1, nx):
        j = (x + i) % nx
        arrived(wx.at[j], wx_s.at[i], wx_r.at[j], to_x(j))
    loads[2].wait()
    for j in range(nx):
        asm[j * rows:(j + 1) * rows, :] = wx[j].astype(F32)

    def wblk(zz):
        return me_dp * nz + zz

    wbuf[wblk(z)] = asm[...].astype(BF16)

    def w_column(zz):
        blk = wbuf.at[wblk(zz)]
        send(blk, blk, wy_s.at[0, zz], wy_r.at[0, zz], to_f)
        send(blk, blk, wy_s.at[1, zz], wy_r.at[1, zz], to_b)

    def w_forward(zz):
        blk = wbuf.at[(yb * CORES + c) * nz + zz]
        arrived(blk, wy_s.at[2, zz], wy_r.at[0, zz], to_f)
        send(blk, blk, wy_s.at[2, zz], wy_r.at[2, zz], to_f)

    def w_group(yy, cc):
        return wbuf.at[pl.ds((yy * CORES + cc) * nz, nz)]

    scan_x_sum(0, ra, tz)
    ring_start(wbuf, wblk, wz_s, wz_r)
    w_column(z)
    ident = lambda zz: zz
    ring_start(tz, ident, sz_s.at[0], sz_r.at[0])

    loads[3].wait()
    causal = (lax.broadcasted_iota(jnp.int32, (tokens, tokens), 0)
              >= lax.broadcasted_iota(jnp.int32, (tokens, tokens), 1))

    def attn_head(h, _):
        a = jnp.where(causal, mm(q[:, cols(h)], k[:, cols(h)], NT), 0.0).astype(BF16)
        attn[h] = a
        outp[:, cols(h)] = mm(a, v[:, cols(h)])
        return 0

    per = HEADS // half
    for n in range(1, half + 1):
        ring_step(tz, ident, sz_s.at[0], sz_r.at[0], n)
        ring_step(wbuf, wblk, wz_s, wz_r, n)
        w_column((z + nz - n) % nz)
        if n < half:
            w_column((z + n) % nz)
        w_forward((z + nz - n + 1) % nz)
        if n > 1:
            w_forward((z + n - 1) % nz)
        if n == half:
            scan_finish(0, ra, tz, po, st, False)
        lax.fori_loop((n - 1) * per, n * per, attn_head, 0)
    send(w_group(y, c), w_group(y, c), wp_s.at[y], wp_r.at[y], to_p)
    w_forward((z + nz - half) % nz)
    send(w_group(yb, c), w_group(yb, c), wp_s.at[yb], wp_r.at[yb], to_p)
    order = [z]
    for n in range(1, half + 1):
        order.append((z + nz - n) % nz)
        if n < half:
            order.append((z + n) % nz)
    for zz in order:
        arrived(wbuf.at[(yf * CORES + c) * nz + zz], wy_s.at[1, zz], wy_r.at[1, zz], to_b)
    send(w_group(yf, c), w_group(yf, c), wp_s.at[yf], wp_r.at[yf], to_p)
    for zz in order:
        arrived(wbuf.at[(y2 * CORES + c) * nz + zz], wy_s.at[2, zz], wy_r.at[2, zz], to_f)
    send(w_group(y2, c), w_group(y2, c), wp_s.at[y2], wp_r.at[y2], to_p)
    loads[4].wait()
    scan_wait(0, st)
    for yy in (y, yb, yf, y2):
        grp = w_group(yy, 1 - c)
        arrived(grp, wp_s.at[yy], wp_r.at[yy], to_p)

    def norm_pair(p, _):
        w2 = wbuf[pl.ds(p * 2 * nz, 2 * nz)].reshape(2 * hd, wbuf.shape[-1])
        ug2 = mm(g[...], w2, NT)
        for i in range(2):
            h = p * 2 + i
            ug = ug2[:, i * hd:(i + 1) * hd]
            qh = q[:, cols(h)]
            o = outp[:, cols(h)] + mm(qh, st[h // hx, h % hx])
            inv = 1.0 / jnp.sqrt(jnp.mean(o * o, axis=-1, keepdims=True) + NORM_EPS)
            normed = o * inv
            gain = gain_ref[pl.ds(h, 1), :]
            unit[:, cols(h)] = (normed * gain).astype(BF16)
            gx[x, pl.ds(h, 1), :] = jnp.sum(ug * normed, axis=0, keepdims=True)
            scaled = ug * gain
            m = jnp.mean(scaled * normed, axis=-1, keepdims=True)
            a = ((scaled - normed * m) * inv).astype(BF16)
            ag[:, cols(h)] = a
            qgs[h // hx, h % hx] = mm(qh, a, TN).astype(BF16)
        return 0

    lax.fori_loop(0, HEADS // 2, norm_pair, 0)

    scan_x_send(1, qgs, rra)
    for i in range(1, nx):
        send(gx.at[x], gx.at[x], gx_s.at[i], gx_r.at[x], to_x((x + i) % nx))

    def wgrad(yy, cc):
        h = yy * CORES + cc
        return mm(unit[:, cols(h)], g[...], TN).reshape(nz, hd // nz, g.shape[-1])

    for yy in (y2, yb, yf, y):
        wgp[yy] = wgrad(yy, 1 - c).astype(BF16)
        send(wgp.at[yy], prt.at[yy], rp_s.at[yy], rp_r.at[yy], to_p)

    def chip_sum(yy):
        own = wgrad(yy, c)
        arrived(prt.at[yy], rp_s.at[yy], rp_r.at[yy], to_p)
        return own + prt[yy].astype(F32)

    zorder = []
    for n in range(half):
        zorder.append((z + half - n) % nz)
        if n < half - 1:
            zorder.append((z + nz - half + 1 + n) % nz)
    zorder.append(z)

    ys2[...] = chip_sum(y2).astype(BF16)
    for zz in zorder:
        send(ys2.at[zz], yr2.at[zz], ry_s.at[0, zz], ry_r.at[0, zz], to_f)
    ysb[...] = chip_sum(yb).astype(BF16)
    for zz in zorder:
        send(ysb.at[zz], yrs.at[zz], ry_s.at[1, zz], ry_r.at[1, zz], to_b)

    scan_x_sum(1, rra, rtz)
    ring_start(rtz, ident, sz_s.at[1], sz_r.at[1])
    for i in range(1, nx):
        j = (x + i) % nx
        arrived(gx.at[j], gx_s.at[i], gx_r.at[j], to_x(j))
    gz[z] = jnp.sum(gx[...], axis=0)
    ring_start(gz, ident, gz_s, gz_r)

    fsum[...] = chip_sum(yf)
    wself[...] = chip_sum(y)

    def y_forward(zz):
        arrived(yr2.at[zz], ry_s.at[0, zz], ry_r.at[0, zz], to_f)
        ysf[zz] = (fsum[zz] + yr2[zz].astype(F32)).astype(BF16)
        send(ysf.at[zz], yrc.at[zz], ry_s.at[2, zz], ry_r.at[2, zz], to_f)

    def grad_head(h, _):
        qh, kh, vh, ah = q[:, cols(h)], k[:, cols(h)], v[:, cols(h)], ag[:, cols(h)]
        sg = jnp.where(causal, mm(ah, vh, NT), 0.0).astype(BF16)
        oq[:, cols(h)] = (mm(sg, kh) + mm(ah, st[h // hx, h % hx], NT)).astype(BF16)
        kpart[:, cols(h)] = mm(sg, qh, TN)
        vpart[:, cols(h)] = mm(attn[h], ah, TN)
        return 0

    for n in range(1, half + 1):
        y_forward(zorder[2 * n - 2])
        y_forward(zorder[2 * n - 1])
        ring_step(rtz, ident, sz_s.at[1], sz_r.at[1], n)
        ring_step(gz, ident, gz_s, gz_r, n)
        if n == half:
            scan_finish(1, rra, rtz, rpo, rst, True)
        lax.fori_loop((n - 1) * per, n * per, grad_head, 0)

    stores = [pltpu.make_async_copy(oq, qo_hbm.at[0], out_s.at[0])]
    stores[0].start()
    gy[y] = jnp.sum(gz[...], axis=0)
    send(gy.at[y], gy.at[y], gy_s.at[0], gy_r.at[0], to_f)
    send(gy.at[y], gy.at[y], gy_s.at[1], gy_r.at[1], to_b)

    def block(zz):
        arrived(yrc.at[zz], ry_s.at[2, zz], ry_r.at[2, zz], to_f)
        arrived(yrs.at[zz], ry_s.at[1, zz], ry_r.at[1, zz], to_b)
        return wself[zz] + yrc[zz].astype(F32) + yrs[zz].astype(F32)

    def z_step(n):
        val = block((z + half - n) % nz)
        if n > 0:
            arrived(zur.at[n - 1], rz_s.at[0, n - 1], rz_r.at[0, n - 1], to_up)
            val = val + zur[n - 1].astype(F32)
        zus[n] = val.astype(BF16)
        send(zus.at[n], zur.at[n], rz_s.at[0, n], rz_r.at[0, n], to_up)
        if n < half - 1:
            val = block((z + nz - half + 1 + n) % nz)
            if n > 0:
                arrived(zdr.at[n - 1], rz_s.at[1, n - 1], rz_r.at[1, n - 1], to_dn)
                val = val + zdr[n - 1].astype(F32)
            zds[n] = val.astype(BF16)
            send(zds.at[n], zdr.at[n], rz_s.at[1, n], rz_r.at[1, n], to_dn)

    z_step(0)
    arrived(gy.at[yb], gy_s.at[0], gy_r.at[0], to_f)
    send(gy.at[yb], gy.at[yb], gy_s.at[2], gy_r.at[2], to_f)

    scan_wait(1, rst)

    def last_head(h, _):
        rev = rst[h // hx, h % hx]
        ok[:, cols(h)] = (kpart[:, cols(h)] + mm(v[:, cols(h)], rev, NT)).astype(BF16)
        ov[:, cols(h)] = (vpart[:, cols(h)] + mm(k[:, cols(h)], rev)).astype(BF16)
        return 0

    lax.fori_loop(0, HEADS, last_head, 0)
    for i, (a, b) in enumerate([(ok, ko_hbm), (ov, vo_hbm)]):
        stores.append(pltpu.make_async_copy(a, b.at[0], out_s.at[i + 1]))
        stores[-1].start()

    for n in range(1, half):
        z_step(n)
    arrived(gy.at[yf], gy_s.at[1], gy_r.at[1], to_b)
    arrived(gy.at[y2], gy_s.at[2], gy_r.at[2], to_f)
    gc[c] = jnp.sum(gy[...], axis=0)
    send(gc.at[c], gc.at[c], gc_s.at[0], gc_r.at[0], to_p)

    fin = block(z)
    arrived(zur.at[half - 1], rz_s.at[0, half - 1], rz_r.at[0, half - 1], to_up)
    fin = fin + zur[half - 1].astype(F32)
    if half > 1:
        arrived(zdr.at[half - 2], rz_s.at[1, half - 2], rz_r.at[1, half - 2], to_dn)
        fin = fin + zdr[half - 2].astype(F32)
    for j in range(nx):
        xs[j] = fin[j * rows:(j + 1) * rows, :]
    for i in range(1, nx):
        j = (x + i) % nx
        send(xs.at[j], xr.at[x], rx_s.at[i], rx_r.at[x], to_x(j))
    xr[x] = xs[x]
    arrived(gc.at[1 - c], gc_s.at[0], gc_r.at[0], to_p)
    go_ref[...] = (gc[0] + gc[1]) * factor
    for i in range(1, nx):
        j = (x + i) % nx
        arrived(xr.at[j], rx_s.at[i], rx_r.at[j], to_x(j))
    wo_ref[...] = jnp.sum(xr[...], axis=0) * factor

    for copy in pending:
        copy.wait_send()
    for store in stores:
        store.wait()


def shards(interpret, queries, keys, values, out_grad, out_weight, gain):
    nx = XDIM
    ndp = lax.axis_size("dp")
    nseq = lax.axis_size("seq")
    nz = nseq // nx
    hx = HEADS // nx
    half = nz // 2
    hd = HEAD_DIM
    tok = queries.shape[1]
    d = out_grad.shape[2]
    width = HEADS * hd
    rows = out_weight.shape[0]
    br = rows * nx
    total = tok * ndp * nseq
    factor = 1.0 / float(total) ** 0.5
    vm = pltpu.VMEM
    dma = pltpu.SemaphoreType.DMA
    blocks = vm((nz, br, d), BF16)
    states = vm((nx, hx, hd, hd), BF16)
    ring = vm((nz, hx, hd, hd), BF16)
    flat = vm((tok, width), BF16)
    flat32 = vm((tok, width), F32)
    dn = max(half - 1, 1)
    scratch = [
        flat, flat, flat, vm((tok, d), BF16), flat, flat, flat,
        vm((nx, rows, d), BF16), vm((br, d), F32), vm((ndp * nz, br, d), BF16),
        vm((HEADS, tok, tok), BF16), flat32, flat, flat, flat32, flat32,
        states, states, ring, states, states, states, states, ring, states, states,
        vm((YDIM, nz, br, d), BF16), vm((YDIM, nz, br, d), BF16),
        blocks, blocks, blocks, blocks, blocks, blocks, vm((nz, br, d), F32), vm((nz, br, d), F32),
        vm((half, br, d), BF16), vm((half, br, d), BF16), vm((dn, br, d), BF16), vm((dn, br, d), BF16),
        vm((nx, rows, d), F32), vm((nx, rows, d), F32),
        vm((nx, HEADS, hd), F32), vm((nz, HEADS, hd), F32), vm((YDIM, HEADS, hd), F32), vm((CORES, HEADS, hd), F32),
        dma((5,)), dma((3,)), dma((nx,)), dma((nx,)), dma((2, half + 1)), dma((nz,)),
        dma((3, nz)), dma((3, nz)), dma((YDIM,)), dma((YDIM,)),
        dma((2, nx)), dma((2, nx)), dma((2, 2, half + 1)), dma((2, nz)), dma((2, nx)), dma((2, nx)),
        dma((YDIM,)), dma((YDIM,)), dma((3, nz)), dma((3, nz)), dma((2, half)), dma((2, half)),
        dma((nx,)), dma((nx,)),
        dma((nx,)), dma((nx,)), dma((2, half + 1)), dma((nz,)), dma((3,)), dma((3,)), dma((1,)), dma((1,)),
    ]
    any_spec = pl.BlockSpec(memory_space=pl.ANY)
    vspec = pl.BlockSpec(memory_space=pltpu.VMEM)
    grad = jax.ShapeDtypeStruct((1, tok, width), BF16)
    flops = 2 * tok * width * (2 * d + 6 * tok + 7 * hd)
    qg, kg, vg, wg, gg = pl.pallas_call(
        functools.partial(kernel, nz, factor),
        out_shape=(grad, grad, grad,
                   jax.ShapeDtypeStruct((rows, d), F32), jax.ShapeDtypeStruct((HEADS, hd), F32)),
        in_specs=[any_spec] * 5 + [vspec],
        out_specs=(any_spec, any_spec, any_spec, vspec, vspec),
        scratch_shapes=scratch,
        compiler_params=pltpu.CompilerParams(
            collective_id=0, has_side_effects=True, vmem_limit_bytes=62 * 1024 * 1024),
        cost_estimate=pl.CostEstimate(flops=flops, bytes_accessed=16 * 1024 * 1024, transcendentals=0),
        interpret=interpret,
    )(queries, keys, values, out_grad, out_weight, gain.reshape(HEADS, hd))
    return qg, kg, vg, wg, gg.reshape(width)


def solution(mesh, interpret=False):
    tokens = P("dp", "seq", None)
    placed = (tokens, tokens, tokens, tokens, P(("dp", "seq"), None), P())
    return jax.shard_map(
        functools.partial(shards, interpret),
        mesh=mesh,
        in_specs=placed,
        out_specs=(tokens, tokens, tokens, P(("dp", "seq"), None), P()),
        check_vma=False,
    )
```

```python
import functools

import jax
import jax.numpy as jnp
from jax import lax
from jax.experimental import pallas as pl
from jax.experimental.pallas import tpu as pltpu
from jax.sharding import PartitionSpec as P

HEADS = 8
HEAD_DIM = 128
NORM_EPS = 1e-06
XDIM = 4
YDIM = 4
CORES = 2
MESH = pl.DeviceIdType.MESH
F32 = jnp.float32
BF16 = jnp.bfloat16

NT = (((1,), (1,)), ((), ()))
TN = (((0,), (0,)), ((), ()))


def mm(a, b, dims=(((1,), (0,)), ((), ()))):
    return lax.dot_general(a, b, dims, preferred_element_type=F32)


def kernel(nz, factor, q_hbm, k_hbm, v_hbm, g_hbm, w_hbm, gain_ref,
           qo_hbm, ko_hbm, vo_hbm, wo_ref, go_ref,
           q, k, v, g, oq, ok, ov, wx, asm, wbuf, attn, outp, inv_ref, unit, ag, kpart, vpart,
           kvs, ra, ts, tr, es, er, po, st, qgs, rra, rts, rtr, res, rer, rpo, rst,
           wgp, prt, ys2, yr2, ysf, yrc, ysb, yrs, fsum, wself, zs, zr, xs, xr, gx, gz, gy, gc,
           in_s, out_s, wx_s, wx_r, wz_s, wz_r, wy_s, wy_r, wp_s, wp_r,
           sx_s, sx_r, sz_s, sz_r, sb_s, sb_r, rp_s, rp_r, ry_s, ry_r, rz_s, rz_r, rx_s, rx_r,
           gx_s, gx_r, gz_s, gz_r, gy_s, gy_r, gc_s, gc_r):
    nx = XDIM
    hx = HEADS // nx
    me_dp = lax.axis_index("dp")
    me_seq = lax.axis_index("seq")
    y = me_dp // CORES
    c = me_dp % CORES
    z = me_seq // nx
    x = me_seq % nx
    step = 1 - 2 * c
    yf = (y + step + YDIM) % YDIM
    yb = (y - step + YDIM) % YDIM
    y2 = (y + 2) % YDIM
    tokens = q.shape[0]
    hd = HEAD_DIM
    rows = wx.shape[1]

    def to_x(j):
        return (me_dp, z * nx + j)

    def to_y(j):
        return (j * CORES + c, me_seq)

    def to_z(j):
        return (me_dp, j * nx + x)

    to_f = to_y(yf)
    to_b = to_y(yb)
    to_p = (y * CORES + 1 - c, me_seq)

    xs_other = [(x + i) % nx for i in ((2, 1, 3) if nx == 4 else range(1, nx))]
    z_offsets = sorted(range(1, nz), key=lambda o: -min(o, nz - o))
    zs_other = [(z + o) % nz for o in z_offsets]

    pending = []

    def send(src, dst, ss, rs, dev):
        copy = pltpu.make_async_remote_copy(
            src_ref=src, dst_ref=dst, send_sem=ss, recv_sem=rs, device_id=dev, device_id_type=MESH)
        copy.start()
        pending.append(copy)

    def arrived(dst, ss, rs, dev):
        pltpu.make_async_remote_copy(
            src_ref=dst, dst_ref=dst, send_sem=ss, recv_sem=rs, device_id=dev, device_id_type=MESH).wait_recv()

    def cols(h):
        return pl.ds(pl.multiple_of(h * hd, hd), hd)

    barrier = pltpu.get_barrier_semaphore()
    peers = [to_z(j) for j in zs_other] + [to_x(j) for j in xs_other] + [to_y(y2), to_f, to_b, to_p]
    for peer in peers:
        pl.semaphore_signal(barrier, inc=1, device_id=peer, device_id_type=MESH)

    loads = [pltpu.make_async_copy(a, b, in_s.at[i]) for i, (a, b) in enumerate(
        [(k_hbm.at[0], k), (v_hbm.at[0], v), (w_hbm, wx.at[x]), (q_hbm.at[0], q), (g_hbm.at[0], g)])]
    for load in loads:
        load.start()

    loads[0].wait()
    loads[1].wait()

    def kv_head(h, _):
        kvs[h // hx, h % hx] = mm(k[:, cols(h)], v[:, cols(h)], TN).astype(BF16)
        return 0

    lax.fori_loop(0, HEADS, kv_head, 0)
    pl.semaphore_wait(barrier, len(peers))

    for i, j in enumerate(xs_other):
        send(w_hbm, wx.at[x], wx_s.at[i], wx_r.at[x], to_x(j))

    def scan_x_send(n, snd, recv):
        for i, j in enumerate(xs_other):
            send(snd.at[j], recv.at[x], sx_s.at[n, i], sx_r.at[n, x], to_x(j))
        recv[x] = snd[x]

    def scan_z_send(n, recv, out, ring):
        for i, j in enumerate(xs_other):
            arrived(recv.at[j], sx_s.at[n, i], sx_r.at[n, j], to_x(j))
        total = recv[0].astype(F32)
        for j in range(1, nx):
            total = total + recv[j].astype(F32)
        total = total.astype(BF16)
        for i in range(hx):
            out[:, i] = total[i].reshape(nz, hd // nz, hd)
        for i, j in enumerate(zs_other):
            send(out.at[j], ring.at[z], sz_s.at[n, 0, i], sz_r.at[n, 0, z], to_z(j))
        ring[z] = out[z]

    def scan_z_back(n, ring, out, back, reverse):
        for i, j in enumerate(zs_other):
            arrived(ring.at[j], sz_s.at[n, 0, i], sz_r.at[n, 0, j], to_z(j))
        acc = jnp.zeros(ring.shape[1:], F32)
        for zz in (range(nz - 1, -1, -1) if reverse else range(nz)):
            out[zz] = acc.astype(BF16)
            acc = acc + ring[zz].astype(F32)
        for i, j in enumerate(zs_other):
            send(out.at[j], back.at[z], sz_s.at[n, 1, i], sz_r.at[n, 1, z], to_z(j))
        back[z] = out[z]

    def scan_x_back(n, recv, back, out, state, reverse):
        for i, j in enumerate(zs_other):
            arrived(back.at[j], sz_s.at[n, 1, i], sz_r.at[n, 1, j], to_z(j))
        for i in range(hx):
            acc = back[:, i].reshape(hd, hd).astype(F32)
            for j in (range(nx - 1, -1, -1) if reverse else range(nx)):
                out[j, i] = acc.astype(BF16)
                acc = acc + recv[j, i].astype(F32)
        for i, j in enumerate(xs_other):
            send(out.at[j], state.at[x], sb_s.at[n, i], sb_r.at[n, x], to_x(j))
        state[x] = out[x]

    def scan_wait(n, state):
        for i, j in enumerate(xs_other):
            arrived(state.at[j], sb_s.at[n, i], sb_r.at[n, j], to_x(j))

    scan_x_send(0, kvs, ra)

    loads[3].wait()
    causal = (lax.broadcasted_iota(jnp.int32, (tokens, tokens), 0)
              >= lax.broadcasted_iota(jnp.int32, (tokens, tokens), 1))

    def attn_head(h, _):
        a = jnp.where(causal, mm(q[:, cols(h)], k[:, cols(h)], NT), 0.0).astype(BF16)
        attn[h] = a
        outp[:, cols(h)] = mm(a, v[:, cols(h)])
        return 0

    lax.fori_loop(0, 2, attn_head, 0)

    for i, j in enumerate(xs_other):
        arrived(wx.at[j], wx_s.at[i], wx_r.at[j], to_x(j))
    loads[2].wait()
    for j in range(nx):
        asm[j * rows:(j + 1) * rows, :] = wx[j].astype(F32)

    def wblk(yy, zz):
        return wbuf.at[(yy * CORES + c) * nz + zz]

    wbuf[me_dp * nz + z] = asm[...].astype(BF16)

    def w_z(zz, offset, slot):
        send(wblk(y, zz), wblk(y, zz), wz_s.at[slot], wz_r.at[zz], to_z((z + offset + nz) % nz))

    def w_z_arrived(zz):
        arrived(wblk(y, zz), wz_s.at[0], wz_r.at[zz], to_p)

    def w_column(zz):
        send(wblk(y, zz), wblk(y, zz), wy_s.at[0, zz], wy_r.at[0, zz], to_f)
        send(wblk(y, zz), wblk(y, zz), wy_s.at[1, zz], wy_r.at[1, zz], to_b)

    def w_forward(zz):
        arrived(wblk(yb, zz), wy_s.at[2, zz], wy_r.at[0, zz], to_f)
        send(wblk(yb, zz), wblk(yb, zz), wy_s.at[2, zz], wy_r.at[2, zz], to_f)

    def w_group(yy, cc):
        return wbuf.at[pl.ds((yy * CORES + cc) * nz, nz)]

    def w_to_core(yy):
        send(w_group(yy, c), w_group(yy, c), wp_s.at[yy], wp_r.at[yy], to_p)

    far = nz == 8
    near = [1, -1, 2, -2] if far else ([1, -1, 2] if nz == 4 else [1])
    for slot, offset in enumerate(near):
        w_z(z, offset, slot)
    w_column(z)

    scan_z_send(0, ra, ts, tr)
    lax.fori_loop(2, 4, attn_head, 0)

    order = [z]
    for offset in near:
        zz = (z - offset + nz) % nz
        w_z_arrived(zz)
        if far and offset == 2:
            w_z(zz, 1, 4)
            w_z(zz, 2, 5)
        if far and offset == -2:
            w_z(zz, -1, 6)
        w_column(zz)
        order.append(zz)
    scan_z_back(0, tr, es, er, False)
    w_forward(z)
    lax.fori_loop(4, 6, attn_head, 0)
    for zz in order[1:]:
        w_forward(zz)
    late = []
    for offset in ([3, -3, 4] if far else []):
        zz = (z - offset + nz) % nz
        w_z_arrived(zz)
        w_column(zz)
        late.append(zz)
    scan_x_back(0, ra, er, po, st, False)
    w_to_core(y)
    lax.fori_loop(6, HEADS, attn_head, 0)
    for zz in late:
        w_forward(zz)
    w_to_core(yb)
    order = order + late
    scan_wait(0, st)

    def norm_head(h, _):
        o = outp[:, cols(h)] + mm(q[:, cols(h)], st[h // hx, h % hx])
        inv = 1.0 / jnp.sqrt(jnp.mean(o * o, axis=-1, keepdims=True) + NORM_EPS)
        normed = o * inv
        inv_ref[h] = inv
        outp[:, cols(h)] = normed
        unit[:, cols(h)] = (normed * gain_ref[pl.ds(h, 1), :]).astype(BF16)
        return 0

    lax.fori_loop(0, HEADS, norm_head, 0)
    loads[4].wait()

    def wgrad(yy, cc):
        h = yy * CORES + cc
        return mm(unit[:, cols(h)], g[...], TN).reshape(nz, hd // nz, g.shape[-1])

    for yy in (y2, yb, yf, y):
        wgp[yy] = wgrad(yy, 1 - c).astype(BF16)
        send(wgp.at[yy], prt.at[yy], rp_s.at[yy], rp_r.at[yy], to_p)

    def chip_sum(yy):
        own = wgrad(yy, c)
        arrived(prt.at[yy], rp_s.at[yy], rp_r.at[yy], to_p)
        return own + prt[yy].astype(F32)

    zorder = [(z + o) % nz for o in z_offsets] + [z]

    ys2[...] = chip_sum(y2).astype(BF16)
    for zz in zorder:
        send(ys2.at[zz], yr2.at[zz], ry_s.at[0, zz], ry_r.at[0, zz], to_f)
    for zz in order:
        arrived(wblk(yf, zz), wy_s.at[1, zz], wy_r.at[1, zz], to_b)
    w_to_core(yf)
    ysb[...] = chip_sum(yb).astype(BF16)
    for zz in zorder:
        send(ysb.at[zz], yrs.at[zz], ry_s.at[1, zz], ry_r.at[1, zz], to_b)
    for zz in order:
        arrived(wblk(y2, zz), wy_s.at[2, zz], wy_r.at[2, zz], to_f)
    w_to_core(y2)
    fsum[...] = chip_sum(yf)
    for yy in (y, yb, yf, y2):
        arrived(w_group(yy, 1 - c), wp_s.at[yy], wp_r.at[yy], to_p)

    def grad_pair(p, _):
        w2 = wbuf[pl.ds(p * 2 * nz, 2 * nz)].reshape(2 * hd, wbuf.shape[-1])
        ug2 = mm(g[...], w2, NT)
        for i in range(2):
            h = p * 2 + i
            ug = ug2[:, i * hd:(i + 1) * hd]
            normed = outp[:, cols(h)]
            gx[x, pl.ds(h, 1), :] = jnp.sum(ug * normed, axis=0, keepdims=True)
            scaled = ug * gain_ref[pl.ds(h, 1), :]
            m = jnp.mean(scaled * normed, axis=-1, keepdims=True)
            a = ((scaled - normed * m) * inv_ref[h]).astype(BF16)
            ag[:, cols(h)] = a
            qgs[h // hx, h % hx] = mm(q[:, cols(h)], a, TN).astype(BF16)
        return 0

    lax.fori_loop(0, HEADS // 2, grad_pair, 0)

    scan_x_send(1, qgs, rra)
    for i, j in enumerate(xs_other):
        send(gx.at[x], gx.at[x], gx_s.at[i], gx_r.at[x], to_x(j))

    def y_forward(zz):
        arrived(yr2.at[zz], ry_s.at[0, zz], ry_r.at[0, zz], to_f)
        ysf[zz] = (fsum[zz] + yr2[zz].astype(F32)).astype(BF16)
        send(ysf.at[zz], yrc.at[zz], ry_s.at[2, zz], ry_r.at[2, zz], to_f)

    def block(zz):
        arrived(yrc.at[zz], ry_s.at[2, zz], ry_r.at[2, zz], to_f)
        arrived(yrs.at[zz], ry_s.at[1, zz], ry_r.at[1, zz], to_b)
        return wself[zz] + yrc[zz].astype(F32) + yrs[zz].astype(F32)

    def z_send(i):
        j = zorder[i]
        zs[j] = block(j).astype(BF16)
        send(zs.at[j], zr.at[z], rz_s.at[i], rz_r.at[z], to_z(j))

    def grad_head(h, _):
        qh, kh, vh, ah = q[:, cols(h)], k[:, cols(h)], v[:, cols(h)], ag[:, cols(h)]
        sg = jnp.where(causal, mm(ah, vh, NT), 0.0).astype(BF16)
        oq[:, cols(h)] = (mm(sg, kh) + mm(ah, st[h // hx, h % hx], NT)).astype(BF16)
        kpart[:, cols(h)] = mm(sg, qh, TN)
        vpart[:, cols(h)] = mm(attn[h], ah, TN)
        return 0

    for zz in zorder:
        y_forward(zz)
    wself[...] = chip_sum(y)
    lax.fori_loop(0, 4, grad_head, 0)

    scan_z_send(1, rra, rts, rtr)
    for i, j in enumerate(xs_other):
        arrived(gx.at[j], gx_s.at[i], gx_r.at[j], to_x(j))
    gz[z] = jnp.sum(gx[...], axis=0)
    for i, j in enumerate(zs_other):
        send(gz.at[z], gz.at[z], gz_s.at[i], gz_r.at[z], to_z(j))

    lax.fori_loop(4, HEADS, grad_head, 0)
    stores = [pltpu.make_async_copy(oq, qo_hbm.at[0], out_s.at[0])]
    stores[0].start()

    scan_z_back(1, rtr, res, rer, True)
    for i, j in enumerate(zs_other):
        arrived(gz.at[j], gz_s.at[i], gz_r.at[j], to_z(j))
    gy[y] = jnp.sum(gz[...], axis=0)
    for i, j in enumerate((y2, yf, yb)):
        send(gy.at[y], gy.at[y], gy_s.at[i], gy_r.at[y], to_y(j))
    early = (nz - 1) // 2
    for i in range(early):
        z_send(i)
    scan_x_back(1, rra, rer, rpo, rst, True)
    for i, j in enumerate((y2, yf, yb)):
        arrived(gy.at[j], gy_s.at[i], gy_r.at[j], to_y(j))
    gc[c] = jnp.sum(gy[...], axis=0)
    send(gc.at[c], gc.at[c], gc_s.at[0], gc_r.at[0], to_p)
    for i in range(early, nz - 1):
        z_send(i)
    fin = block(z)

    scan_wait(1, rst)

    def last_head(h, _):
        rev = rst[h // hx, h % hx]
        ok[:, cols(h)] = (kpart[:, cols(h)] + mm(v[:, cols(h)], rev, NT)).astype(BF16)
        ov[:, cols(h)] = (vpart[:, cols(h)] + mm(k[:, cols(h)], rev)).astype(BF16)
        return 0

    lax.fori_loop(0, HEADS, last_head, 0)
    for i, (a, b) in enumerate([(ok, ko_hbm), (ov, vo_hbm)]):
        stores.append(pltpu.make_async_copy(a, b.at[0], out_s.at[i + 1]))
        stores[-1].start()

    for i, j in enumerate(zs_other):
        arrived(zr.at[j], rz_s.at[i], rz_r.at[j], to_z(j))
        fin = fin + zr[j].astype(F32)
    for j in range(nx):
        xs[j] = fin[j * rows:(j + 1) * rows, :]
    for i, j in enumerate(xs_other):
        send(xs.at[j], xr.at[x], rx_s.at[i], rx_r.at[x], to_x(j))
    xr[x] = xs[x]
    arrived(gc.at[1 - c], gc_s.at[0], gc_r.at[0], to_p)
    go_ref[...] = (gc[0] + gc[1]) * factor
    for i, j in enumerate(xs_other):
        arrived(xr.at[j], rx_s.at[i], rx_r.at[j], to_x(j))
    wo_ref[...] = jnp.sum(xr[...], axis=0) * factor

    for copy in pending:
        copy.wait_send()
    for store in stores:
        store.wait()


def place(*refs):
    n = (len(refs) - 2) // 3
    src, dst, buf = refs[:n], refs[n:2 * n], refs[2 * n:3 * n]
    in_s, out_s = refs[3 * n:]
    loads = [pltpu.make_async_copy(src[i], buf[i], in_s.at[i]) for i in range(n)]
    stores = [pltpu.make_async_copy(buf[i], dst[i], out_s.at[i]) for i in range(n)]
    for load in loads:
        load.start()
    for load, store in zip(loads, stores):
        load.wait()
        store.start()
    for store in stores:
        store.wait()


def shards(interpret, queries, keys, values, out_grad, out_weight, gain):
    nx = XDIM
    ndp = lax.axis_size("dp")
    nseq = lax.axis_size("seq")
    nz = nseq // nx
    hx = HEADS // nx
    hd = HEAD_DIM
    tok = queries.shape[1]
    d = out_grad.shape[2]
    width = HEADS * hd
    rows = out_weight.shape[0]
    br = rows * nx
    total = tok * ndp * nseq
    factor = 1.0 / float(total) ** 0.5
    vm = pltpu.VMEM
    dma = pltpu.SemaphoreType.DMA
    blocks = vm((nz, br, d), BF16)
    states = vm((nx, hx, hd, hd), BF16)
    ring = vm((nz, hx, hd // nz, hd), BF16)
    flat = vm((tok, width), BF16)
    flat32 = vm((tok, width), F32)
    scan = [states, states, ring, ring, ring, ring, states, states]
    other = max(nx - 1, 1)
    scratch = [
        flat, flat, flat, vm((tok, d), BF16), flat, flat, flat,
        vm((nx, rows, d), BF16), vm((br, d), F32), vm((ndp * nz, br, d), BF16),
        vm((HEADS, tok, tok), BF16), flat32, vm((HEADS, tok, 1), F32), flat, flat, flat32, flat32,
        *scan, *scan,
        vm((YDIM, nz, br, d), BF16), vm((YDIM, nz, br, d), BF16),
        blocks, blocks, blocks, blocks, blocks, blocks, vm((nz, br, d), F32), vm((nz, br, d), F32),
        blocks, blocks, vm((nx, rows, d), F32), vm((nx, rows, d), F32),
        vm((nx, HEADS, hd), F32), vm((nz, HEADS, hd), F32), vm((YDIM, HEADS, hd), F32), vm((CORES, HEADS, hd), F32),
        dma((5,)), dma((3,)), dma((other,)), dma((nx,)), dma((7,)), dma((nz,)),
        dma((3, nz)), dma((3, nz)), dma((YDIM,)), dma((YDIM,)),
        dma((2, other)), dma((2, nx)), dma((2, 2, nz)), dma((2, 2, nz)), dma((2, other)), dma((2, nx)),
        dma((YDIM,)), dma((YDIM,)), dma((3, nz)), dma((3, nz)), dma((nz,)), dma((nz,)),
        dma((other,)), dma((nx,)),
        dma((other,)), dma((nx,)), dma((nz,)), dma((nz,)), dma((3,)), dma((YDIM,)), dma((1,)), dma((1,)),
    ]
    any_spec = pl.BlockSpec(memory_space=pl.ANY)
    vspec = pl.BlockSpec(memory_space=pltpu.VMEM)
    grad = jax.ShapeDtypeStruct((1, tok, width), BF16)
    flops = 2 * tok * width * (2 * d + 6 * tok + 7 * hd)
    shapes = (grad, grad, grad,
              jax.ShapeDtypeStruct((rows, d), F32), jax.ShapeDtypeStruct((HEADS, hd), F32))
    parts = pl.pallas_call(
        functools.partial(kernel, nz, factor),
        out_shape=shapes,
        in_specs=[any_spec] * 5 + [vspec],
        out_specs=(any_spec, any_spec, any_spec, vspec, vspec),
        scratch_shapes=scratch,
        compiler_params=pltpu.CompilerParams(
            collective_id=0, has_side_effects=True, vmem_limit_bytes=62 * 1024 * 1024),
        cost_estimate=pl.CostEstimate(flops=flops, bytes_accessed=16 * 1024 * 1024, transcendentals=0),
        interpret=interpret,
    )(queries, keys, values, out_grad, out_weight, gain.reshape(HEADS, hd))
    qg, kg, vg, wg, gg = pl.pallas_call(
        place,
        out_shape=shapes,
        in_specs=[any_spec] * 5,
        out_specs=(any_spec,) * 5,
        scratch_shapes=[vm(s.shape, s.dtype) for s in shapes] + [dma((5,)), dma((5,))],
        compiler_params=pltpu.CompilerParams(vmem_limit_bytes=62 * 1024 * 1024),
        interpret=interpret,
    )(*parts)
    return qg, kg, vg, wg, gg.reshape(width)


def solution(mesh, interpret=False):
    tokens = P("dp", "seq", None)
    placed = (tokens, tokens, tokens, tokens, P(("dp", "seq"), None), P())
    return jax.shard_map(
        functools.partial(shards, interpret),
        mesh=mesh,
        in_specs=placed,
        out_specs=(tokens, tokens, tokens, P(("dp", "seq"), None), P()),
        check_vma=False,
    )
```

```python
import functools

import jax
import jax.numpy as jnp
from jax import lax
from jax.experimental import pallas as pl
from jax.experimental.pallas import tpu as pltpu
from jax.sharding import PartitionSpec as P

HEADS = 8
HEAD_DIM = 128
NORM_EPS = 1e-06
XDIM = 4
YDIM = 4
CORES = 2
MESH = pl.DeviceIdType.MESH
F32 = jnp.float32
BF16 = jnp.bfloat16

NT = (((1,), (1,)), ((), ()))
TN = (((0,), (0,)), ((), ()))


def mm(a, b, dims=(((1,), (0,)), ((), ()))):
    return lax.dot_general(a, b, dims, preferred_element_type=F32)


def kernel(nz, factor, q_hbm, k_hbm, v_hbm, g_hbm, w_hbm, gain_ref,
           oq, ok, ov, wo_ref, go_ref,
           q, k, v, g, wx, asm, wbuf, attn, outp, inv_ref, unit, ag, kpart, vpart,
           kvs, ra, ts, tr, es, er, po, st, qgs, rra, rts, rtr, res, rer, rpo, rst,
           wgp, prt, ysend, yrecv, ysum, ysf, yrc, zs, zr, zf, xs, xr, gx, gz, gy, gc,
           in_s, wx_s, wx_r, wz_s, wz_r, wy_s, wy_r, wp_s, wp_r,
           sx_s, sx_r, sz_s, sz_r, sb_s, sb_r, rp_s, rp_r, ry_s, ry_r, rz_s, rz_r, rf_r, rx_s, rx_r,
           gx_s, gx_r, gz_s, gz_r, gy_s, gy_r, gc_s, gc_r):
    nx = XDIM
    hx = HEADS // nx
    me_dp = lax.axis_index("dp")
    me_seq = lax.axis_index("seq")
    y = me_dp // CORES
    c = me_dp % CORES
    z = me_seq // nx
    x = me_seq % nx
    step = 1 - 2 * c
    yf = (y + step + YDIM) % YDIM
    yb = (y - step + YDIM) % YDIM
    y2 = (y + 2) % YDIM
    tokens = q.shape[0]
    hd = HEAD_DIM
    rows = wx.shape[1]

    def to_x(j):
        return (me_dp, z * nx + j)

    def to_y(j):
        return (j * CORES + c, me_seq)

    def to_z(j):
        return (me_dp, j * nx + x)

    to_f = to_y(yf)
    to_b = to_y(yb)
    to_p = (y * CORES + 1 - c, me_seq)

    x_offsets = [2, 1, 3] if nx == 4 else list(range(1, nx))
    xs_other = [(x + i) % nx for i in x_offsets]
    z_offsets = sorted(range(1, nz), key=lambda o: -min(o, nz - o))
    zs_other = [(z + o) % nz for o in z_offsets]

    def send(src, dst, ss, rs, dev):
        copy = pltpu.make_async_remote_copy(
            src_ref=src, dst_ref=dst, send_sem=ss, recv_sem=rs, device_id=dev, device_id_type=MESH)
        copy.start()

    def arrived(dst, ss, rs, dev):
        pltpu.make_async_remote_copy(
            src_ref=dst, dst_ref=dst, send_sem=ss, recv_sem=rs, device_id=dev, device_id_type=MESH).wait_recv()

    def heads_loop(body, steps):
        def one(h, _):
            for at, run in steps:
                pl.when(h == at)(run)
            body(h, 0)
            return 0

        lax.fori_loop(0, HEADS, one, 0)

    def cols(h):
        return pl.ds(pl.multiple_of(h * hd, hd), hd)

    barrier = pltpu.get_barrier_semaphore()
    peers = [to_z(j) for j in zs_other] + [to_x(j) for j in xs_other] + [to_y(y2), to_f, to_b, to_p]
    for peer in peers:
        pl.semaphore_signal(barrier, inc=1, device_id=peer, device_id_type=MESH)

    loads = [pltpu.make_async_copy(a, b, in_s.at[i]) for i, (a, b) in enumerate(
        [(k_hbm.at[0], k), (v_hbm.at[0], v), (w_hbm, wx.at[x]), (q_hbm.at[0], q), (g_hbm.at[0], g)])]
    for load in loads:
        load.start()

    loads[0].wait()
    loads[1].wait()

    def kv_head(h, _):
        kvs[h // hx, h % hx] = mm(k[:, cols(h)], v[:, cols(h)], TN).astype(BF16)
        return 0

    lax.fori_loop(0, HEADS, kv_head, 0)
    pl.semaphore_wait(barrier, len(peers))

    for i, j in enumerate(xs_other):
        send(w_hbm, wx.at[x], wx_s.at[i], wx_r.at[x], to_x(j))

    def scan_x_send(n, snd, recv):
        for i, j in enumerate(xs_other):
            send(snd.at[j], recv.at[x], sx_s.at[n, i], sx_r.at[n, x], to_x(j))
        recv[x] = snd[x]

    def scan_z_send(n, recv, out, ring):
        for i, j in enumerate(xs_other):
            arrived(recv.at[j], sx_s.at[n, i], sx_r.at[n, j], to_x(j))
        total = recv[0].astype(F32)
        for j in range(1, nx):
            total = total + recv[j].astype(F32)
        total = total.astype(BF16)
        for i in range(hx):
            out[:, i] = total[i].reshape(nz, hd // nz, hd)
        for i, j in enumerate(zs_other):
            send(out.at[j], ring.at[z], sz_s.at[n, 0, i], sz_r.at[n, 0, z], to_z(j))
        ring[z] = out[z]

    def scan_z_back(n, ring, out, back, reverse):
        for i, j in enumerate(zs_other):
            arrived(ring.at[j], sz_s.at[n, 0, i], sz_r.at[n, 0, j], to_z(j))
        acc = jnp.zeros(ring.shape[1:], F32)
        for zz in (range(nz - 1, -1, -1) if reverse else range(nz)):
            out[zz] = acc.astype(BF16)
            acc = acc + ring[zz].astype(F32)
        for i, j in enumerate(zs_other):
            send(out.at[j], back.at[z], sz_s.at[n, 1, i], sz_r.at[n, 1, z], to_z(j))
        back[z] = out[z]

    def scan_x_back(n, recv, back, out, state, reverse):
        for i, j in enumerate(zs_other):
            arrived(back.at[j], sz_s.at[n, 1, i], sz_r.at[n, 1, j], to_z(j))
        for i in range(hx):
            acc = back[:, i].reshape(hd, hd).astype(F32)
            for j in (range(nx - 1, -1, -1) if reverse else range(nx)):
                out[j, i] = acc.astype(BF16)
                acc = acc + recv[j, i].astype(F32)
        for i, j in enumerate(xs_other):
            send(out.at[j], state.at[x], sb_s.at[n, i], sb_r.at[n, x], to_x(j))
        state[x] = out[x]

    def scan_wait(n, state):
        for i, j in enumerate(xs_other):
            arrived(state.at[j], sb_s.at[n, i], sb_r.at[n, j], to_x(j))

    scan_x_send(0, kvs, ra)

    loads[3].wait()
    causal = (lax.broadcasted_iota(jnp.int32, (tokens, tokens), 0)
              >= lax.broadcasted_iota(jnp.int32, (tokens, tokens), 1))

    def attn_head(h, _):
        a = jnp.where(causal, mm(q[:, cols(h)], k[:, cols(h)], NT), 0.0).astype(BF16)
        attn[h] = a
        outp[:, cols(h)] = mm(a, v[:, cols(h)])
        return 0

    def wblk(yy, zz):
        return wbuf.at[(yy * CORES + c) * nz + zz]

    def w_z(zz, offset, slot):
        send(wblk(y, zz), wblk(y, zz), wz_s.at[slot], wz_r.at[zz], to_z((z + offset + nz) % nz))

    def w_z_arrived(zz):
        arrived(wblk(y, zz), wz_s.at[0], wz_r.at[zz], to_p)

    def w_column(zz):
        send(wblk(y, zz), wblk(y, zz), wy_s.at[0, zz], wy_r.at[0, zz], to_f)
        send(wblk(y, zz), wblk(y, zz), wy_s.at[1, zz], wy_r.at[1, zz], to_b)

    def w_forward(zz):
        arrived(wblk(yb, zz), wy_s.at[2, zz], wy_r.at[0, zz], to_f)
        send(wblk(yb, zz), wblk(yb, zz), wy_s.at[2, zz], wy_r.at[2, zz], to_f)

    def w_group(yy, cc):
        return wbuf.at[pl.ds((yy * CORES + cc) * nz, nz)]

    def w_to_core(yy):
        send(w_group(yy, c), w_group(yy, c), wp_s.at[yy], wp_r.at[yy], to_p)

    far = nz == 8
    near = [1, -1, 2, -2] if far else ([1, -1, 2] if nz == 4 else [1])
    order = [z] + [(z - o + nz) % nz for o in near]
    late = [(z - o + nz) % nz for o in ([3, -3, 4] if far else [])]

    def w_rows():
        for i, j in enumerate(xs_other):
            arrived(wx.at[j], wx_s.at[i], wx_r.at[j], to_x(j))
        loads[2].wait()
        for j in range(nx):
            asm[j * rows:(j + 1) * rows, :] = wx[j].astype(F32)
        wbuf[me_dp * nz + z] = asm[...].astype(BF16)
        for slot, offset in enumerate(near):
            w_z(z, offset, slot)
        w_column(z)

    def w_near():
        for offset, zz in zip(near, order[1:]):
            w_z_arrived(zz)
            if far and offset == 2:
                w_z(zz, 1, 4)
            if far and offset == -2:
                w_z(zz, -1, 6)
                w_z((z - 2 * step + nz) % nz, 2 * step, 5)
            w_column(zz)

    def w_far():
        for zz in late:
            w_z_arrived(zz)
            w_column(zz)

    def w_forwards(some):
        for zz in some:
            w_forward(zz)

    heads_loop(attn_head, [
        (2, w_rows),
        (3, lambda: scan_z_send(0, ra, ts, tr)),
        (4, w_near),
        (6, lambda: scan_z_back(0, tr, es, er, False)),
        (6, lambda: w_forwards(order)),
        (7, w_far),
    ])
    scan_x_back(0, ra, er, po, st, False)
    w_to_core(y)
    w_forwards(late)
    w_to_core(yb)
    order = order + late
    scan_wait(0, st)

    def norm_head(h, _):
        o = outp[:, cols(h)] + mm(q[:, cols(h)], st[h // hx, h % hx])
        inv = 1.0 / jnp.sqrt(jnp.mean(o * o, axis=-1, keepdims=True) + NORM_EPS)
        normed = o * inv
        inv_ref[h] = inv
        outp[:, cols(h)] = normed
        unit[:, cols(h)] = (normed * gain_ref[pl.ds(h, 1), :]).astype(BF16)
        return 0

    loads[4].wait()

    def wgrad(yy, cc):
        h = yy * CORES + cc
        norm_head(h, 0)
        return mm(unit[:, cols(h)], g[...], TN).reshape(nz, hd // nz, g.shape[-1])

    def ring_y(i):
        return (y + 2 + step * i + 2 * YDIM) % YDIM

    def to_partner(i, _):
        yy = ring_y(i)
        wgp[yy] = wgrad(yy, 1 - c).astype(BF16)
        send(wgp.at[yy], prt.at[yy], rp_s.at[yy], rp_r.at[yy], to_p)
        return 0

    lax.fori_loop(0, YDIM, to_partner, 0)

    def chip_sum(yy):
        own = wgrad(yy, c)
        arrived(prt.at[yy], rp_s.at[yy], rp_r.at[yy], to_p)
        return own + prt[yy].astype(F32)

    def y_forward(zz):
        arrived(yrecv.at[0, zz], ry_s.at[0, zz], ry_r.at[0, zz], to_f)
        ysf[zz] = (ysum[1, zz] + yrecv[0, zz].astype(F32)).astype(BF16)
        send(ysf.at[zz], yrc.at[zz], ry_s.at[2, zz], ry_r.at[2, zz], to_f)

    if far:
        z_targets = [4, 3, -3, 2 * step, -2 * step, 1, -1]
        zorder = [(z + o + nz) % nz for o in z_targets] + [z]
        z_first = [(2 * step, 1), (1, 0), (-1, 2)]
    else:
        zorder = [(z + o) % nz for o in z_offsets] + [z]

    def to_ring(i, _):
        total = chip_sum(ring_y(i))

        @pl.when(i < 2)
        def _():
            ysend[i] = total.astype(BF16)
            for zz in zorder:
                send(ysend.at[i, zz], yrecv.at[i, zz], ry_s.at[i, zz], ry_r.at[i, zz],
                     to_y((y + step * (1 - 2 * i) + YDIM) % YDIM))

        @pl.when(i >= 2)
        def _():
            ysum[i - 2] = total

        @pl.when(i == 0)
        def _():
            for zz in order:
                arrived(wblk(yf, zz), wy_s.at[1, zz], wy_r.at[1, zz], to_b)
            w_to_core(yf)

        @pl.when(i == 2)
        def _():
            for zz in order:
                arrived(wblk(y2, zz), wy_s.at[2, zz], wy_r.at[2, zz], to_f)
            w_to_core(y2)

        return 0

    lax.fori_loop(0, YDIM, to_ring, 0)
    cut = nz // 4
    for zz in zorder[:2 * cut]:
        y_forward(zz)
    for yy in (y, yb, yf, y2):
        arrived(w_group(yy, 1 - c), wp_s.at[yy], wp_r.at[yy], to_p)

    def grad_pair(p, _):
        w2 = wbuf[pl.ds(p * 2 * nz, 2 * nz)].reshape(2 * hd, wbuf.shape[-1])
        ug2 = mm(g[...], w2, NT)
        for i in range(2):
            h = p * 2 + i
            ug = ug2[:, i * hd:(i + 1) * hd]
            normed = outp[:, cols(h)]
            gx[x, pl.ds(h, 1), :] = jnp.sum(ug * normed, axis=0, keepdims=True)
            scaled = ug * gain_ref[pl.ds(h, 1), :]
            m = jnp.mean(scaled * normed, axis=-1, keepdims=True)
            a = ((scaled - normed * m) * inv_ref[h]).astype(BF16)
            ag[:, cols(h)] = a
            qgs[h // hx, h % hx] = mm(q[:, cols(h)], a, TN).astype(BF16)
        return 0

    todo = zorder[2 * cut:]
    def some_pairs(i, _):
        p = (x + 1 + i) % nx
        for j in range(hx // 2):
            grad_pair(p * (hx // 2) + j, 0)

        @pl.when(i < nx - 1)
        def _():
            send(qgs.at[p], rra.at[x], sx_s.at[1, i], sx_r.at[1, x], to_x(p))

        for at in range(nx):
            @pl.when(i == at)
            def _():
                for zz in todo[len(todo) * at // nx:len(todo) * (at + 1) // nx]:
                    y_forward(zz)

        return 0

    lax.fori_loop(0, nx, some_pairs, 0)
    rra[x] = qgs[x]

    for i, j in enumerate(xs_other):
        send(gx.at[x], gx.at[x], gx_s.at[i], gx_r.at[x], to_x(j))

    def block(zz):
        arrived(yrc.at[zz], ry_s.at[2, zz], ry_r.at[2, zz], to_f)
        arrived(yrecv.at[1, zz], ry_s.at[1, zz], ry_r.at[1, zz], to_b)
        return ysum[0, zz] + yrc[zz].astype(F32) + yrecv[1, zz].astype(F32)

    def z_share(n):
        arrived(zf.at[n], rz_s.at[0], rf_r.at[n], to_p)
        return zf[n].astype(F32)

    def z_send(i):
        j = zorder[i]
        total = block(j)
        if far and i < 3:
            offset, n = z_first[i]
            zs[j] = total.astype(BF16)
            send(zs.at[j], zf.at[n], rz_s.at[i], rf_r.at[n], to_z((z + offset + nz) % nz))
            return
        if far and i == 3:
            total = total + z_share(1) + z_share(1 - step)
        if far and i == 4:
            total = total + z_share(1 + step)
        zs[j] = total.astype(BF16)
        send(zs.at[j], zr.at[z], rz_s.at[i], rz_r.at[z], to_z(j))

    def grad_head(h, _):
        qh, kh, vh, ah = q[:, cols(h)], k[:, cols(h)], v[:, cols(h)], ag[:, cols(h)]
        sg = jnp.where(causal, mm(ah, vh, NT), 0.0).astype(BF16)
        oq[0, :, cols(h)] = (mm(sg, kh) + mm(ah, st[h // hx, h % hx], NT)).astype(BF16)
        kpart[:, cols(h)] = mm(sg, qh, TN)
        vpart[:, cols(h)] = mm(attn[h], ah, TN)
        return 0

    def z_sends(first, upto):
        for i in range(first, min(upto, nz - 1)):
            z_send(i)

    def gain_z():
        for i, j in enumerate(xs_other):
            arrived(gx.at[j], gx_s.at[i], gx_r.at[j], to_x(j))
        gz[z] = jnp.sum(gx[...], axis=0)
        for i, j in enumerate(zs_other):
            send(gz.at[z], gz.at[z], gz_s.at[i], gz_r.at[z], to_z(j))

    def gain_y():
        for i, j in enumerate(zs_other):
            arrived(gz.at[j], gz_s.at[i], gz_r.at[j], to_z(j))
        gy[y] = jnp.sum(gz[...], axis=0)
        for i, j in enumerate((y2, yf, yb)):
            send(gy.at[y], gy.at[y], gy_s.at[i], gy_r.at[y], to_y(j))

    heads_loop(grad_head, [
        (2, lambda: z_sends(0, 1)),
        (4, lambda: scan_z_send(1, rra, rts, rtr)),
        (4, gain_z),
        (4, lambda: z_sends(1, 3)),
        (6, lambda: z_sends(3, 4)),
        (7, lambda: scan_z_back(1, rtr, res, rer, True)),
        (7, gain_y),
        (7, lambda: z_sends(4, 6)),
    ])
    z_sends(6, nz)
    scan_x_back(1, rra, rer, rpo, rst, True)
    for i, j in enumerate((y2, yf, yb)):
        arrived(gy.at[j], gy_s.at[i], gy_r.at[j], to_y(j))
    gc[c] = jnp.sum(gy[...], axis=0)
    send(gc.at[c], gc.at[c], gc_s.at[0], gc_r.at[0], to_p)
    fin = block(z)

    for j in ([(z + o + nz) % nz for o in near] if far else zs_other):
        arrived(zr.at[j], rz_s.at[0], rz_r.at[j], to_z(j))
        fin = fin + zr[j].astype(F32)
    for j in range(nx):
        xs[j] = fin[j * rows:(j + 1) * rows, :]
    for i, j in enumerate(xs_other):
        send(xs.at[j], xr.at[x], rx_s.at[i], rx_r.at[x], to_x(j))
    xr[x] = xs[x]

    scan_wait(1, rst)

    def last_head(h, _):
        rev = rst[h // hx, h % hx]
        ok[0, :, cols(h)] = (kpart[:, cols(h)] + mm(v[:, cols(h)], rev, NT)).astype(BF16)
        ov[0, :, cols(h)] = (vpart[:, cols(h)] + mm(k[:, cols(h)], rev)).astype(BF16)
        return 0

    lax.fori_loop(0, HEADS, last_head, 0)

    arrived(gc.at[1 - c], gc_s.at[0], gc_r.at[0], to_p)
    go_ref[...] = (gc[0] + gc[1]) * factor
    for i, j in enumerate(xs_other):
        arrived(xr.at[j], rx_s.at[i], rx_r.at[j], to_x(j))
    wo_ref[...] = jnp.sum(xr[...], axis=0) * factor

    def left(src, ss):
        pltpu.make_async_remote_copy(
            src_ref=src, dst_ref=src, send_sem=ss, recv_sem=ss, device_id=to_p, device_id_type=MESH).wait_send()

    for i in range(nx - 1):
        for src, ss in ((w_hbm, wx_s.at[i]), (kvs.at[0], sx_s.at[0, i]), (qgs.at[0], sx_s.at[1, i]),
                        (po.at[0], sb_s.at[0, i]), (rpo.at[0], sb_s.at[1, i]),
                        (gx.at[0], gx_s.at[i]), (xs.at[0], rx_s.at[i])):
            left(src, ss)
    for i in range(nz - 1):
        for n in range(2):
            left(ts.at[0], sz_s.at[n, 0, i])
            left(ts.at[0], sz_s.at[n, 1, i])
        left(gz.at[0], gz_s.at[i])
        left(zs.at[0], rz_s.at[i])
    for i in range(len(near) + len(late)):
        left(wbuf.at[0], wz_s.at[i])
    for i in range(3):
        for zz in range(nz):
            left(wbuf.at[0], wy_s.at[i, zz])
            left(ysf.at[0], ry_s.at[i, zz])
        left(gy.at[0], gy_s.at[i])
    for yy in range(YDIM):
        left(w_group(0, 0), wp_s.at[yy])
        left(wgp.at[0], rp_s.at[yy])
    left(gc.at[0], gc_s.at[0])


def place(*refs):
    n = len(refs) // 2
    stores = [pltpu.make_async_copy(refs[i], refs[n + i], refs[2 * n].at[i]) for i in range(n)]
    for store in stores:
        store.start()
    for store in stores:
        store.wait()


def shards(interpret, queries, keys, values, out_grad, out_weight, gain):
    nx = XDIM
    ndp = lax.axis_size("dp")
    nseq = lax.axis_size("seq")
    nz = nseq // nx
    hx = HEADS // nx
    hd = HEAD_DIM
    tok = queries.shape[1]
    d = out_grad.shape[2]
    width = HEADS * hd
    rows = out_weight.shape[0]
    br = rows * nx
    total = tok * ndp * nseq
    factor = 1.0 / float(total) ** 0.5
    vm = pltpu.VMEM
    dma = pltpu.SemaphoreType.DMA
    blocks = vm((nz, br, d), BF16)
    states = vm((nx, hx, hd, hd), BF16)
    ring = vm((nz, hx, hd // nz, hd), BF16)
    flat = vm((tok, width), BF16)
    flat32 = vm((tok, width), F32)
    scan = [states, states, ring, ring, ring, ring, states, states]
    other = max(nx - 1, 1)
    scratch = [
        flat, flat, flat, vm((tok, d), BF16),
        vm((nx, rows, d), BF16), vm((br, d), F32), vm((ndp * nz, br, d), BF16),
        vm((HEADS, tok, tok), BF16), flat32, vm((HEADS, tok, 1), F32), flat, flat, flat32, flat32,
        *scan, *scan,
        vm((YDIM, nz, br, d), BF16), vm((YDIM, nz, br, d), BF16),
        vm((2, nz, br, d), BF16), vm((2, nz, br, d), BF16), vm((2, nz, br, d), F32), blocks, blocks,
        blocks, blocks, vm((3, br, d), BF16), vm((nx, rows, d), F32), vm((nx, rows, d), F32),
        vm((nx, HEADS, hd), F32), vm((nz, HEADS, hd), F32), vm((YDIM, HEADS, hd), F32), vm((CORES, HEADS, hd), F32),
        dma((5,)), dma((other,)), dma((nx,)), dma((7,)), dma((nz,)),
        dma((3, nz)), dma((3, nz)), dma((YDIM,)), dma((YDIM,)),
        dma((2, other)), dma((2, nx)), dma((2, 2, nz)), dma((2, 2, nz)), dma((2, other)), dma((2, nx)),
        dma((YDIM,)), dma((YDIM,)), dma((3, nz)), dma((3, nz)), dma((nz,)), dma((nz,)), dma((3,)),
        dma((other,)), dma((nx,)),
        dma((other,)), dma((nx,)), dma((nz,)), dma((nz,)), dma((3,)), dma((YDIM,)), dma((1,)), dma((1,)),
    ]
    any_spec = pl.BlockSpec(memory_space=pl.ANY)
    vspec = pl.BlockSpec(memory_space=pltpu.VMEM)
    grad = jax.ShapeDtypeStruct((1, tok, width), BF16)
    flops = 2 * tok * width * (2 * d + 6 * tok + 7 * hd)
    shapes = (grad, grad, grad,
              jax.ShapeDtypeStruct((rows, d), F32), jax.ShapeDtypeStruct((HEADS, hd), F32))
    parts = pl.pallas_call(
        functools.partial(kernel, nz, factor),
        out_shape=shapes,
        in_specs=[any_spec] * 5 + [vspec],
        out_specs=(vspec,) * 5,
        scratch_shapes=scratch,
        compiler_params=pltpu.CompilerParams(
            collective_id=0, has_side_effects=True, vmem_limit_bytes=51600 * 1 * 1024),
        cost_estimate=pl.CostEstimate(flops=flops, bytes_accessed=16 * 1024 * 1024, transcendentals=0),
        interpret=interpret,
    )(queries, keys, values, out_grad, out_weight, gain.reshape(HEADS, hd))
    qg, kg, vg, wg, gg = pl.pallas_call(
        place,
        out_shape=shapes,
        in_specs=[vspec] * 5,
        out_specs=(any_spec,) * 5,
        scratch_shapes=[dma((5,))],
        compiler_params=pltpu.CompilerParams(vmem_limit_bytes=8 * 1024 * 1024),
        interpret=interpret,
    )(*parts)
    return qg, kg, vg, wg, gg.reshape(width)


def solution(mesh, interpret=False):
    tokens = P("dp", "seq", None)
    placed = (tokens, tokens, tokens, tokens, P(("dp", "seq"), None), P())
    return jax.shard_map(
        functools.partial(shards, interpret),
        mesh=mesh,
        in_specs=placed,
        out_specs=(tokens, tokens, tokens, P(("dp", "seq"), None), P()),
        check_vma=False,
    )
```

```python
import functools

import jax
import jax.numpy as jnp
from jax import lax
from jax.experimental import pallas as pl
from jax.experimental.pallas import tpu as pltpu
from jax.sharding import PartitionSpec as P

HEADS = 8
HEAD_DIM = 128
NORM_EPS = 1e-06
XDIM = 4
YDIM = 4
CORES = 2
MESH = pl.DeviceIdType.MESH
F32 = jnp.float32
BF16 = jnp.bfloat16

NT = (((1,), (1,)), ((), ()))
TN = (((0,), (0,)), ((), ()))


def mm(a, b, dims=(((1,), (0,)), ((), ()))):
    return lax.dot_general(a, b, dims, preferred_element_type=F32)


def kernel(nz, factor, q_hbm, k_hbm, v_hbm, g_hbm, w_hbm, gain_ref,
           oq, ok, ov, wo_ref, go_ref,
           q, k, v, g, wx, asm, wbuf, attn, outp, inv_ref, unit, ag, kpart, vpart,
           kvs, ra, ts, tr, es, er, po, st, qgs, rra, rts, rtr, res, rer, rpo, rst,
           wgp, prt, ysend, yrecv, ysum, ysf, yrc, zs, zr, zf, xs, xr, gx, gz, gy, gc,
           in_s, wx_s, wx_r, wz_s, wz_r, wy_s, wy_r, wp_s, wp_r,
           sx_s, sx_r, sz_s, sz_r, sb_s, sb_r, rp_s, rp_r, ry_s, ry_r, rz_s, rz_r, rf_r, rx_s, rx_r,
           gx_s, gx_r, gz_s, gz_r, gy_s, gy_r, gc_s, gc_r):
    nx = XDIM
    hx = HEADS // nx
    me_dp = lax.axis_index("dp")
    me_seq = lax.axis_index("seq")
    y = me_dp // CORES
    c = me_dp % CORES
    z = me_seq // nx
    x = me_seq % nx
    step = 1 - 2 * c
    yf = (y + step + YDIM) % YDIM
    yb = (y - step + YDIM) % YDIM
    y2 = (y + 2) % YDIM
    tokens = q.shape[0]
    hd = HEAD_DIM
    rows = wx.shape[1]

    def to_x(j):
        return (me_dp, z * nx + j)

    def to_y(j):
        return (j * CORES + c, me_seq)

    def to_z(j):
        return (me_dp, j * nx + x)

    to_f = to_y(yf)
    to_b = to_y(yb)
    to_p = (y * CORES + 1 - c, me_seq)

    x_offsets = [2, 1, 3] if nx == 4 else list(range(1, nx))
    xs_other = [(x + i) % nx for i in x_offsets]
    z_offsets = sorted(range(1, nz), key=lambda o: -min(o, nz - o))
    zs_other = [(z + o) % nz for o in z_offsets]

    def send(src, dst, ss, rs, dev):
        copy = pltpu.make_async_remote_copy(
            src_ref=src, dst_ref=dst, send_sem=ss, recv_sem=rs, device_id=dev, device_id_type=MESH)
        copy.start()

    def arrived(dst, ss, rs, dev):
        pltpu.make_async_remote_copy(
            src_ref=dst, dst_ref=dst, send_sem=ss, recv_sem=rs, device_id=dev, device_id_type=MESH).wait_recv()

    def heads_loop(body, steps):
        def one(h, _):
            for at, run in steps:
                pl.when(h == at)(run)
            body(h, 0)
            return 0

        lax.fori_loop(0, HEADS, one, 0)

    def cols(h):
        return pl.ds(pl.multiple_of(h * hd, hd), hd)

    barrier = pltpu.get_barrier_semaphore()
    peers = [to_z(j) for j in zs_other] + [to_x(j) for j in xs_other] + [to_y(y2), to_f, to_b, to_p]
    for peer in peers:
        pl.semaphore_signal(barrier, inc=1, device_id=peer, device_id_type=MESH)

    loads = [pltpu.make_async_copy(a, b, in_s.at[i]) for i, (a, b) in enumerate(
        [(k_hbm.at[0], k), (v_hbm.at[0], v), (w_hbm, wx.at[x]), (q_hbm.at[0], q), (g_hbm.at[0], g)])]
    for load in loads:
        load.start()

    loads[0].wait()
    loads[1].wait()

    def kv_head(h, _):
        kvs[h // hx, h % hx] = mm(k[:, cols(h)], v[:, cols(h)], TN).astype(BF16)
        return 0

    lax.fori_loop(0, HEADS, kv_head, 0)
    pl.semaphore_wait(barrier, len(peers))

    for i, j in enumerate(xs_other):
        send(w_hbm, wx.at[x], wx_s.at[i], wx_r.at[x], to_x(j))

    def scan_x_send(n, snd, recv):
        for i, j in enumerate(xs_other):
            send(snd.at[j], recv.at[x], sx_s.at[n, i], sx_r.at[n, x], to_x(j))
        recv[x] = snd[x]

    def scan_z_send(n, recv, out, ring):
        for i, j in enumerate(xs_other):
            arrived(recv.at[j], sx_s.at[n, i], sx_r.at[n, j], to_x(j))
        total = recv[0].astype(F32)
        for j in range(1, nx):
            total = total + recv[j].astype(F32)
        total = total.astype(BF16)
        for i in range(hx):
            out[:, i] = total[i].reshape(nz, hd // nz, hd)
        for i, j in enumerate(zs_other):
            send(out.at[j], ring.at[z], sz_s.at[n, 0, i], sz_r.at[n, 0, z], to_z(j))
        ring[z] = out[z]

    def scan_z_back(n, ring, out, back, reverse):
        for i, j in enumerate(zs_other):
            arrived(ring.at[j], sz_s.at[n, 0, i], sz_r.at[n, 0, j], to_z(j))
        acc = jnp.zeros(ring.shape[1:], F32)
        for zz in (range(nz - 1, -1, -1) if reverse else range(nz)):
            out[zz] = acc.astype(BF16)
            acc = acc + ring[zz].astype(F32)
        for i, j in enumerate(zs_other):
            send(out.at[j], back.at[z], sz_s.at[n, 1, i], sz_r.at[n, 1, z], to_z(j))
        back[z] = out[z]

    def scan_x_back(n, recv, back, out, state, reverse):
        for i, j in enumerate(zs_other):
            arrived(back.at[j], sz_s.at[n, 1, i], sz_r.at[n, 1, j], to_z(j))
        for i in range(hx):
            acc = back[:, i].reshape(hd, hd).astype(F32)
            for j in (range(nx - 1, -1, -1) if reverse else range(nx)):
                out[j, i] = acc.astype(BF16)
                acc = acc + recv[j, i].astype(F32)
        for i, j in enumerate(xs_other):
            send(out.at[j], state.at[x], sb_s.at[n, i], sb_r.at[n, x], to_x(j))
        state[x] = out[x]

    def scan_wait(n, state):
        for i, j in enumerate(xs_other):
            arrived(state.at[j], sb_s.at[n, i], sb_r.at[n, j], to_x(j))

    scan_x_send(0, kvs, ra)

    loads[3].wait()
    causal = (lax.broadcasted_iota(jnp.int32, (tokens, tokens), 0)
              >= lax.broadcasted_iota(jnp.int32, (tokens, tokens), 1))

    def attn_head(h, _):
        a = jnp.where(causal, mm(q[:, cols(h)], k[:, cols(h)], NT), 0.0).astype(BF16)
        attn[h] = a
        outp[:, cols(h)] = mm(a, v[:, cols(h)])
        return 0

    def wblk(yy, zz):
        return wbuf.at[(yy * CORES + c) * nz + zz]

    def w_z(zz, offset, slot):
        send(wblk(y, zz), wblk(y, zz), wz_s.at[slot], wz_r.at[zz], to_z((z + offset + nz) % nz))

    def w_z_arrived(zz):
        arrived(wblk(y, zz), wz_s.at[0], wz_r.at[zz], to_p)

    def w_column(zz):
        send(wblk(y, zz), wblk(y, zz), wy_s.at[0, zz], wy_r.at[0, zz], to_f)
        send(wblk(y, zz), wblk(y, zz), wy_s.at[1, zz], wy_r.at[1, zz], to_b)

    def w_forward(zz):
        arrived(wblk(yb, zz), wy_s.at[2, zz], wy_r.at[0, zz], to_f)
        send(wblk(yb, zz), wblk(yb, zz), wy_s.at[2, zz], wy_r.at[2, zz], to_f)

    def w_group(yy, cc):
        return wbuf.at[pl.ds((yy * CORES + cc) * nz, nz)]

    def w_to_core(yy):
        send(w_group(yy, c), w_group(yy, c), wp_s.at[yy], wp_r.at[yy], to_p)

    far = nz == 8
    near = [1, -1, 2, -2] if far else ([1, -1, 2] if nz == 4 else [1])
    order = [z] + [(z - o + nz) % nz for o in near]
    late = [(z - o + nz) % nz for o in ([3, -3, 4] if far else [])]

    def w_rows():
        for i, j in enumerate(xs_other):
            arrived(wx.at[j], wx_s.at[i], wx_r.at[j], to_x(j))
        loads[2].wait()
        for j in range(nx):
            asm[j * rows:(j + 1) * rows, :] = wx[j].astype(F32)
        wbuf[me_dp * nz + z] = asm[...].astype(BF16)
        for slot, offset in enumerate(near):
            w_z(z, offset, slot)
        w_column(z)

    def w_near():
        for offset, zz in zip(near, order[1:]):
            w_z_arrived(zz)
            if far and offset == 2:
                w_z(zz, 1, 4)
            if far and offset == -2:
                w_z(zz, -1, 6)
                w_z((z - 2 * step + nz) % nz, 2 * step, 5)
            w_column(zz)

    def w_far():
        for zz in late:
            w_z_arrived(zz)
            w_column(zz)

    def w_forwards(some):
        for zz in some:
            w_forward(zz)

    heads_loop(attn_head, [
        (2, w_rows),
        (3, lambda: scan_z_send(0, ra, ts, tr)),
        (4, w_near),
        (6, lambda: scan_z_back(0, tr, es, er, False)),
        (6, w_far),
        (6, lambda: w_forwards(order)),
    ])
    scan_x_back(0, ra, er, po, st, False)
    w_to_core(y)
    w_forwards(late)
    w_to_core(yb)
    order = order + late
    scan_wait(0, st)

    def norm_head(h, _):
        o = outp[:, cols(h)] + mm(q[:, cols(h)], st[h // hx, h % hx])
        inv = 1.0 / jnp.sqrt(jnp.mean(o * o, axis=-1, keepdims=True) + NORM_EPS)
        normed = o * inv
        inv_ref[h] = inv
        outp[:, cols(h)] = normed
        unit[:, cols(h)] = (normed * gain_ref[pl.ds(h, 1), :]).astype(BF16)
        return 0

    loads[4].wait()

    def wgrad(yy, cc):
        h = yy * CORES + cc
        norm_head(h, 0)
        return mm(unit[:, cols(h)], g[...], TN).reshape(nz, hd // nz, g.shape[-1])

    def ring_y(i):
        return (y + 2 + step * i + 2 * YDIM) % YDIM

    def to_partner(i, _):
        yy = ring_y(i)
        wgp[yy] = wgrad(yy, 1 - c).astype(BF16)
        send(wgp.at[yy], prt.at[yy], rp_s.at[yy], rp_r.at[yy], to_p)
        return 0

    lax.fori_loop(0, YDIM, to_partner, 0)

    def chip_sum(yy):
        own = wgrad(yy, c)
        arrived(prt.at[yy], rp_s.at[yy], rp_r.at[yy], to_p)
        return own + prt[yy].astype(F32)

    def y_forward(zz):
        arrived(yrecv.at[0, zz], ry_s.at[0, zz], ry_r.at[0, zz], to_f)
        ysf[zz] = (ysum[1, zz] + yrecv[0, zz].astype(F32)).astype(BF16)
        send(ysf.at[zz], yrc.at[zz], ry_s.at[2, zz], ry_r.at[2, zz], to_f)

    if far:
        z_targets = [4, 3, -3, 2 * step, -2 * step, 1, -1]
        zorder = [(z + o + nz) % nz for o in z_targets] + [z]
        z_first = [(2 * step, 1), (1, 0), (-1, 2)]
    else:
        zorder = [(z + o) % nz for o in z_offsets] + [z]

    def to_ring(i, _):
        total = chip_sum(ring_y(i))

        @pl.when(i < 2)
        def _():
            ysend[i] = total.astype(BF16)
            for zz in zorder:
                send(ysend.at[i, zz], yrecv.at[i, zz], ry_s.at[i, zz], ry_r.at[i, zz],
                     to_y((y + step * (1 - 2 * i) + YDIM) % YDIM))

        @pl.when(i >= 2)
        def _():
            ysum[i - 2] = total

        @pl.when(i == 0)
        def _():
            for zz in order:
                arrived(wblk(yf, zz), wy_s.at[1, zz], wy_r.at[1, zz], to_b)
            w_to_core(yf)

        @pl.when(i == 2)
        def _():
            for zz in order:
                arrived(wblk(y2, zz), wy_s.at[2, zz], wy_r.at[2, zz], to_f)
            w_to_core(y2)

        return 0

    lax.fori_loop(0, YDIM, to_ring, 0)
    cut = nz // 4
    for zz in zorder[:2 * cut]:
        y_forward(zz)
    for yy in (y, yb, yf, y2):
        arrived(w_group(yy, 1 - c), wp_s.at[yy], wp_r.at[yy], to_p)

    def grad_pair(p, _):
        w2 = wbuf[pl.ds(p * 2 * nz, 2 * nz)].reshape(2 * hd, wbuf.shape[-1])
        ug2 = mm(g[...], w2, NT)
        for i in range(2):
            h = p * 2 + i
            ug = ug2[:, i * hd:(i + 1) * hd]
            normed = outp[:, cols(h)]
            gx[x, pl.ds(h, 1), :] = jnp.sum(ug * normed, axis=0, keepdims=True)
            scaled = ug * gain_ref[pl.ds(h, 1), :]
            m = jnp.mean(scaled * normed, axis=-1, keepdims=True)
            a = ((scaled - normed * m) * inv_ref[h]).astype(BF16)
            ag[:, cols(h)] = a
            qgs[h // hx, h % hx] = mm(q[:, cols(h)], a, TN).astype(BF16)
        return 0

    todo = zorder[2 * cut:]
    def some_pairs(i, _):
        p = (x + 1 + i) % nx
        for j in range(hx // 2):
            grad_pair(p * (hx // 2) + j, 0)

        @pl.when(i < nx - 1)
        def _():
            send(qgs.at[p], rra.at[x], sx_s.at[1, i], sx_r.at[1, x], to_x(p))

        for at in range(nx):
            @pl.when(i == at)
            def _():
                for zz in todo[len(todo) * at // nx:len(todo) * (at + 1) // nx]:
                    y_forward(zz)

        return 0

    lax.fori_loop(0, nx, some_pairs, 0)
    rra[x] = qgs[x]

    for i, j in enumerate(xs_other):
        send(gx.at[x], gx.at[x], gx_s.at[i], gx_r.at[x], to_x(j))

    def block(zz):
        arrived(yrc.at[zz], ry_s.at[2, zz], ry_r.at[2, zz], to_f)
        arrived(yrecv.at[1, zz], ry_s.at[1, zz], ry_r.at[1, zz], to_b)
        return ysum[0, zz] + yrc[zz].astype(F32) + yrecv[1, zz].astype(F32)

    def z_share(n):
        arrived(zf.at[n], rz_s.at[0], rf_r.at[n], to_p)
        return zf[n].astype(F32)

    def z_send(i):
        j = zorder[i]
        total = block(j)
        if far and i < 3:
            offset, n = z_first[i]
            zs[j] = total.astype(BF16)
            send(zs.at[j], zf.at[n], rz_s.at[i], rf_r.at[n], to_z((z + offset + nz) % nz))
            return
        if far and i == 3:
            total = total + z_share(1) + z_share(1 - step)
        if far and i == 4:
            total = total + z_share(1 + step)
        zs[j] = total.astype(BF16)
        send(zs.at[j], zr.at[z], rz_s.at[i], rz_r.at[z], to_z(j))

    def grad_head(h, _):
        qh, kh, vh, ah = q[:, cols(h)], k[:, cols(h)], v[:, cols(h)], ag[:, cols(h)]
        sg = jnp.where(causal, mm(ah, vh, NT), 0.0).astype(BF16)
        oq[0, :, cols(h)] = (mm(sg, kh) + mm(ah, st[h // hx, h % hx], NT)).astype(BF16)
        kpart[:, cols(h)] = mm(sg, qh, TN)
        vpart[:, cols(h)] = mm(attn[h], ah, TN)
        return 0

    def z_sends(first, upto):
        for i in range(first, min(upto, nz - 1)):
            z_send(i)

    def gain_z():
        for i, j in enumerate(xs_other):
            arrived(gx.at[j], gx_s.at[i], gx_r.at[j], to_x(j))
        gz[z] = jnp.sum(gx[...], axis=0)
        for i, j in enumerate(zs_other):
            send(gz.at[z], gz.at[z], gz_s.at[i], gz_r.at[z], to_z(j))

    def gain_y():
        for i, j in enumerate(zs_other):
            arrived(gz.at[j], gz_s.at[i], gz_r.at[j], to_z(j))
        gy[y] = jnp.sum(gz[...], axis=0)
        for i, j in enumerate((y2, yf, yb)):
            send(gy.at[y], gy.at[y], gy_s.at[i], gy_r.at[y], to_y(j))

    heads_loop(grad_head, [
        (2, lambda: z_sends(0, 1)),
        (4, lambda: scan_z_send(1, rra, rts, rtr)),
        (4, gain_z),
        (4, lambda: z_sends(1, 3)),
        (6, lambda: z_sends(3, 4)),
        (7, lambda: scan_z_back(1, rtr, res, rer, True)),
        (7, gain_y),
        (7, lambda: z_sends(4, 6)),
    ])
    z_sends(6, nz)
    scan_x_back(1, rra, rer, rpo, rst, True)
    for i, j in enumerate((y2, yf, yb)):
        arrived(gy.at[j], gy_s.at[i], gy_r.at[j], to_y(j))
    gc[c] = jnp.sum(gy[...], axis=0)
    send(gc.at[c], gc.at[c], gc_s.at[0], gc_r.at[0], to_p)
    fin = block(z)

    for j in ([(z + o + nz) % nz for o in near] if far else zs_other):
        arrived(zr.at[j], rz_s.at[0], rz_r.at[j], to_z(j))
        fin = fin + zr[j].astype(F32)
    for j in range(nx):
        xs[j] = fin[j * rows:(j + 1) * rows, :]
    for i, j in enumerate(xs_other):
        send(xs.at[j], xr.at[x], rx_s.at[i], rx_r.at[x], to_x(j))
    xr[x] = xs[x]

    scan_wait(1, rst)

    def last_head(h, _):
        rev = rst[h // hx, h % hx]
        ok[0, :, cols(h)] = (kpart[:, cols(h)] + mm(v[:, cols(h)], rev, NT)).astype(BF16)
        ov[0, :, cols(h)] = (vpart[:, cols(h)] + mm(k[:, cols(h)], rev)).astype(BF16)
        return 0

    lax.fori_loop(0, HEADS, last_head, 0)

    arrived(gc.at[1 - c], gc_s.at[0], gc_r.at[0], to_p)
    go_ref[...] = (gc[0] + gc[1]) * factor
    for i, j in enumerate(xs_other):
        arrived(xr.at[j], rx_s.at[i], rx_r.at[j], to_x(j))
    wo_ref[...] = jnp.sum(xr[...], axis=0) * factor

    def left(src, ss):
        pltpu.make_async_remote_copy(
            src_ref=src, dst_ref=src, send_sem=ss, recv_sem=ss, device_id=to_p, device_id_type=MESH).wait_send()

    for i in range(nx - 1):
        for src, ss in ((w_hbm, wx_s.at[i]), (kvs.at[0], sx_s.at[0, i]), (qgs.at[0], sx_s.at[1, i]),
                        (po.at[0], sb_s.at[0, i]), (rpo.at[0], sb_s.at[1, i]),
                        (gx.at[0], gx_s.at[i]), (xs.at[0], rx_s.at[i])):
            left(src, ss)
    for i in range(nz - 1):
        for n in range(2):
            left(ts.at[0], sz_s.at[n, 0, i])
            left(ts.at[0], sz_s.at[n, 1, i])
        left(gz.at[0], gz_s.at[i])
        left(zs.at[0], rz_s.at[i])
    for i in range(len(near) + len(late)):
        left(wbuf.at[0], wz_s.at[i])
    for i in range(3):
        for zz in range(nz):
            left(wbuf.at[0], wy_s.at[i, zz])
            left(ysf.at[0], ry_s.at[i, zz])
        left(gy.at[0], gy_s.at[i])
    for yy in range(YDIM):
        left(w_group(0, 0), wp_s.at[yy])
        left(wgp.at[0], rp_s.at[yy])
    left(gc.at[0], gc_s.at[0])


def place(*refs):
    n = len(refs) // 2
    stores = [pltpu.make_async_copy(refs[i], refs[n + i], refs[2 * n].at[i]) for i in range(n)]
    for store in stores:
        store.start()
    for store in stores:
        store.wait()


def shards(interpret, queries, keys, values, out_grad, out_weight, gain):
    nx = XDIM
    ndp = lax.axis_size("dp")
    nseq = lax.axis_size("seq")
    nz = nseq // nx
    hx = HEADS // nx
    hd = HEAD_DIM
    tok = queries.shape[1]
    d = out_grad.shape[2]
    width = HEADS * hd
    rows = out_weight.shape[0]
    br = rows * nx
    total = tok * ndp * nseq
    factor = 1.0 / float(total) ** 0.5
    vm = pltpu.VMEM
    dma = pltpu.SemaphoreType.DMA
    blocks = vm((nz, br, d), BF16)
    states = vm((nx, hx, hd, hd), BF16)
    ring = vm((nz, hx, hd // nz, hd), BF16)
    flat = vm((tok, width), BF16)
    flat32 = vm((tok, width), F32)
    scan = [states, states, ring, ring, ring, ring, states, states]
    other = max(nx - 1, 1)
    scratch = [
        flat, flat, flat, vm((tok, d), BF16),
        vm((nx, rows, d), BF16), vm((br, d), F32), vm((ndp * nz, br, d), BF16),
        vm((HEADS, tok, tok), BF16), flat32, vm((HEADS, tok, 1), F32), flat, flat, flat32, flat32,
        *scan, *scan,
        vm((YDIM, nz, br, d), BF16), vm((YDIM, nz, br, d), BF16),
        vm((2, nz, br, d), BF16), vm((2, nz, br, d), BF16), vm((2, nz, br, d), F32), blocks, blocks,
        blocks, blocks, vm((3, br, d), BF16), vm((nx, rows, d), F32), vm((nx, rows, d), F32),
        vm((nx, HEADS, hd), F32), vm((nz, HEADS, hd), F32), vm((YDIM, HEADS, hd), F32), vm((CORES, HEADS, hd), F32),
        dma((5,)), dma((other,)), dma((nx,)), dma((7,)), dma((nz,)),
        dma((3, nz)), dma((3, nz)), dma((YDIM,)), dma((YDIM,)),
        dma((2, other)), dma((2, nx)), dma((2, 2, nz)), dma((2, 2, nz)), dma((2, other)), dma((2, nx)),
        dma((YDIM,)), dma((YDIM,)), dma((3, nz)), dma((3, nz)), dma((nz,)), dma((nz,)), dma((3,)),
        dma((other,)), dma((nx,)),
        dma((other,)), dma((nx,)), dma((nz,)), dma((nz,)), dma((3,)), dma((YDIM,)), dma((1,)), dma((1,)),
    ]
    any_spec = pl.BlockSpec(memory_space=pl.ANY)
    vspec = pl.BlockSpec(memory_space=pltpu.VMEM)
    grad = jax.ShapeDtypeStruct((1, tok, width), BF16)
    flops = 2 * tok * width * (2 * d + 6 * tok + 7 * hd)
    shapes = (grad, grad, grad,
              jax.ShapeDtypeStruct((rows, d), F32), jax.ShapeDtypeStruct((HEADS, hd), F32))
    parts = pl.pallas_call(
        functools.partial(kernel, nz, factor),
        out_shape=shapes,
        in_specs=[any_spec] * 5 + [vspec],
        out_specs=(vspec,) * 5,
        scratch_shapes=scratch,
        compiler_params=pltpu.CompilerParams(
            collective_id=0, has_side_effects=True, vmem_limit_bytes=51600 * 1 * 1024),
        cost_estimate=pl.CostEstimate(flops=flops, bytes_accessed=16 * 1024 * 1024, transcendentals=0),
        interpret=interpret,
    )(queries, keys, values, out_grad, out_weight, gain.reshape(HEADS, hd))
    qg, kg, vg, wg, gg = pl.pallas_call(
        place,
        out_shape=shapes,
        in_specs=[vspec] * 5,
        out_specs=(any_spec,) * 5,
        scratch_shapes=[dma((5,))],
        compiler_params=pltpu.CompilerParams(vmem_limit_bytes=8 * 1024 * 1024),
        interpret=interpret,
    )(*parts)
    return qg, kg, vg, wg, gg.reshape(width)


def solution(mesh, interpret=False):
    tokens = P("dp", "seq", None)
    placed = (tokens, tokens, tokens, tokens, P(("dp", "seq"), None), P())
    return jax.shard_map(
        functools.partial(shards, interpret),
        mesh=mesh,
        in_specs=placed,
        out_specs=(tokens, tokens, tokens, P(("dp", "seq"), None), P()),
        check_vma=False,
    )
```
